32 devices in a mesh: plane: 4 (over z), tile: 8 (over y, x, core).
Axes of the slice: x: 2, y: 2, z: 4, core: 2. Of those that a mesh axis runs over, the one named last changes fastest.
Arguments:
- block_dest: int32 [4, 512, 1], P('plane', 'tile'), may hold values from 0 to 7; in each aligned block of 64 rows (0 to 63, 64 to 127, ..., all dimensions but the last counted through in order) at most 16 rows name the same one
- particle_cell: int32 [4, 512, 128], P('plane', 'tile'), may hold values from 0 to 32767, as said below
- particle_offset: float32 [4, 2, 512, 128], P('plane', None, 'tile'), may hold values from 0 to 1
- particle_mass: float32 [4, 512, 128], P('plane', 'tile'), may hold values from -6.7 to 6.7
- ray_cell: int32 [4, 16384], P(None, 'tile'), may hold values from 0 to 32767
- ray_offset: float32 [2, 4, 16384], P(None, None, 'tile'), may hold values from 0 to 1
Outputs:
- lens_fields: float32 [4, 5, 512, 512], P('plane', None, 'tile')
- ray_maps: float32 [4, 4, 6, 16384], P('plane', None, None, 'tile')
The draws below stay inside these ranges and needn't reach their ends.
Inputs may be any that keep to these rules, and one draw needn't show every extreme that they name: `block_dest`: among the blocks of one device (aligned runs of 64 rows), at most 16 name the same tile, and in every draw some device names some tile exactly 16 times. `particle_cell`: Row-major cell index within the 64 x 512 cells of the block's tile. `ray_cell`: Row-major cell index within the 64 x 512 cells of the ray's own tile.
All inputs are finite; a program needn't handle non-finite values.
Results may differ from the reference program's by a relative error of at most 0.0003.
Values sent between devices are 32-bit elements; how exact they have to be, the bound alone decides.
No kernel may reach another device: no remote copies, remote signals or barrier semaphores. Data moves between devices by JAX's collectives and lax.ppermute only.
A program may use at most 64 MiB of HBM per device.

```python
import math
import jax
import jax.numpy as jnp
import numpy as np
from jax import lax

NG = 512
NP = 1024
BLK = 128
BLOCKS_DEV = 64
RAYS = 2048
NB = 4
PLANES = 4
TILES = 8
RT = 64
CAP = 16


def common_cells(key):
    return jax.random.randint(jax.random.fold_in(key, 11), (PLANES, TILES * BLOCKS_DEV, BLK), 0, RT * NG, dtype=jnp.int32)


def draw_particle_cell(key, part):
    return common_cells(key)


def draw_particle_mass(key, part):
    cells = common_cells(key)
    rows = (cells // NG).astype(jnp.float32)
    cols = (cells % NG).astype(jnp.float32)
    phases = jax.random.uniform(jax.random.fold_in(key, 12), (2, PLANES, 1, 1), jnp.float32, -math.pi, math.pi)
    col_wave = 1.5 * jnp.cos(cols * (2.0 * math.pi * 5.0 / NG) + phases[0])
    row_wave = 1.2 * jnp.cos(rows * (2.0 * math.pi / RT) + phases[1])
    noise_key = jax.random.fold_in(key, 13)
    noise = jax.random.truncated_normal(noise_key, -4.0, 4.0, (PLANES, TILES * BLOCKS_DEV, BLK), jnp.float32)
    return (col_wave + row_wave + noise).astype(jnp.float32)


def plant(values, own_key, low, largest):
    extent = values.shape
    index_at = [jax.random.randint(jax.random.fold_in(own_key, axis), (), 0, extent[axis]) for axis in range(len(extent))]
    values = values.at[tuple(index_at)].set(low)
    longest = extent.index(max(extent))
    index_at[longest] = (index_at[longest] + 1) % extent[longest]
    return values.at[tuple(index_at)].set(largest)


def level_of(key, shape, cuts, least, top_value):
    def one(axis_at, parts):
        heights = jax.random.uniform(jax.random.fold_in(jax.random.fold_in(key, 6), axis_at), (parts,), jnp.float32, least / len(cuts), top_value / len(cuts))
        return jnp.repeat(jnp.exp(heights), shape[axis_at] // parts).reshape((-1,) + (1,) * (len(shape) - axis_at - 1))

    loudness = one(*cuts[0])
    for cut in cuts[1:]:
        loudness = loudness * one(*cut)
    return loudness


def assign_block(rng, own, number, rows, count, top, bound, lean):
    ranking = jax.random.permutation(rng, count)
    crowded, ordinary = load_shares(count, rows * top, bound, lean, True), load_shares(count, rows * top, bound, lean, False)
    places = jnp.arange(count)

    def named(tallies, offset_by):
        used = int((tallies > 0).sum())
        fixed = max(1, used // 4)
        moved = fixed + (places - fixed + offset_by * (used - fixed)) % max(1, count - fixed)
        return jnp.zeros((count,), jnp.int32).at[ranking[jnp.where(places < fixed, places, moved)]].set(jnp.asarray(tallies, jnp.int32))

    tallies = jnp.where(number % 4 == 0, named(crowded, number // 4), named(ordinary, number - number // 4 - 1))
    mixed = jax.random.permutation(jax.random.fold_in(own, 3), count)
    source_of, receiver = mixed[0:count // 2 * 2:2], mixed[1:count // 2 * 2:2]
    room = jnp.minimum(tallies[source_of] - 1, bound - tallies[receiver]) // 2
    room = jnp.where((source_of == ranking[0]) | (receiver == ranking[0]) | (tallies[receiver] == 0), 0, jnp.maximum(room, 0))
    moved = jax.random.randint(jax.random.fold_in(own, 4), (count // 2,), 0, 1 << 20) % (room + 1)
    tallies = tallies.at[source_of].add(-moved).at[receiver].add(moved)
    labels = jnp.searchsorted(jnp.cumsum(tallies), jnp.arange(rows * top), side="right").astype(jnp.int32)
    listing = labels.reshape(top, rows).T
    listing = listing[jax.random.permutation(jax.random.fold_in(own, 1), rows)]
    offset_by = jax.random.randint(jax.random.fold_in(own, 2), (rows, 1), 0, top)
    return jnp.take_along_axis(listing, (jnp.arange(top)[None, :] + offset_by) % top, axis=1)


def load_shares(number_of, total, limit, lean, full):
    loads = [(1 << 20) // math.isqrt(standing ** lean) + 1 for standing in range(1, number_of + 1)]
    largest = limit if full else min(limit, max(-(-total // number_of), total * loads[0] // sum(loads)))
    least = 1 if total - largest >= number_of - 1 else 0
    counts, surplus = [largest] + [least] * (number_of - 1), total - largest - least * (number_of - 1)
    while surplus > 0:
        movable = [i for i in range(1, number_of) if counts[i] < largest] or [i for i in range(1, number_of) if counts[i] < limit]
        mass, budget = sum([loads[i] for i in movable]), surplus
        for i in movable:
            extra = min(limit - counts[i], max(1, budget * loads[i] // mass), surplus)
            counts[i] = counts[i] + extra
            surplus = surplus - extra
    return np.array(counts)


def setup_inputs(seed: int = 0) -> dict:
    key_of = jax.random.split(jax.random.key(seed), 7)
    block_dest_keys = jax.random.split(jax.random.fold_in(key_of[0], 1), PLANES * (TILES * BLOCKS_DEV) // BLOCKS_DEV)
    block_dest_turns = jax.random.permutation(jax.random.fold_in(key_of[0], 3), PLANES * (TILES * BLOCKS_DEV) // BLOCKS_DEV)
    block_dest = jax.vmap(lambda own, number: assign_block(jax.random.fold_in(key_of[0], 2), own, number, BLOCKS_DEV, TILES, 1, CAP, 2))(block_dest_keys, block_dest_turns).reshape((PLANES, TILES * BLOCKS_DEV, 1))
    particle_cell = draw_particle_cell(jax.random.fold_in(key_of[6], 71), 0)
    particle_offset = jnp.clip(1.0 * jax.random.uniform(key_of[2], (PLANES, 2, TILES * BLOCKS_DEV, BLK), jnp.float32) ** level_of(key_of[2], (PLANES, 2, TILES * BLOCKS_DEV, BLK), ((0, 4), (2, 8)), -0.2, 0.2), 0.0, 1.0)
    particle_mass = draw_particle_mass(jax.random.fold_in(key_of[6], 71), 0)
    ray_cell = plant(jax.random.randint(key_of[4], (NB, TILES * RAYS), 0, RT * NG), jax.random.fold_in(key_of[4], 1), 0, (RT * NG) - 1).astype(jnp.int32)
    ray_offset = jnp.clip(1.0 * jax.random.uniform(key_of[5], (2, NB, TILES * RAYS), jnp.float32) ** level_of(key_of[5], (2, NB, TILES * RAYS), ((2, 8),), -0.2, 0.2), 0.0, 1.0)
    return {"block_dest": block_dest, "particle_cell": particle_cell, "particle_offset": particle_offset, "particle_mass": particle_mass, "ray_cell": ray_cell, "ray_offset": ray_offset}


LENS_WEIGHT = 0.15
SCREEN_SCALE = 0.5

def wavenumbers(length):
    counter = jnp.arange(length, dtype=jnp.int32)
    signed = jnp.where(counter < length // 2, counter, counter - length)
    return signed.astype(jnp.float32) * (2.0 * jnp.pi / length)

def deposit_plane(targets, cell_ids, offsets, masses):
    tile_rows = NG // TILES
    row_ids = targets[:, None] * tile_rows + cell_ids // NG
    col_ids = cell_ids % NG
    frac_row = offsets[0]
    frac_col = offsets[1]
    canvas = jnp.zeros((NG + 1, NG + 1), jnp.float32)
    canvas = canvas.at[row_ids, col_ids].add(masses * (1.0 - frac_row) * (1.0 - frac_col))
    canvas = canvas.at[row_ids, col_ids + 1].add(masses * (1.0 - frac_row) * frac_col)
    canvas = canvas.at[row_ids + 1, col_ids].add(masses * frac_row * (1.0 - frac_col))
    canvas = canvas.at[row_ids + 1, col_ids + 1].add(masses * frac_row * frac_col)
    scaling = jnp.sqrt(jnp.float32(tile_rows * NG) / jnp.float32(BLOCKS_DEV * BLK))
    return canvas[:NG, :NG] * scaling

def plane_fields(density):
    padded = jnp.zeros((NP, NP), jnp.float32).at[:NG, :NG].set(density)
    spectrum = jnp.fft.fft2(padded)
    wave_x = wavenumbers(NP)[:, None]
    wave_y = wavenumbers(NP)[None, :]
    screen = (SCREEN_SCALE * 2.0 * jnp.pi / NP) ** 2
    potential = spectrum * (-2.0 / (wave_x * wave_x + wave_y * wave_y + screen))
    spectra = [1j * wave_x * potential, 1j * wave_y * potential, -wave_x * wave_x * potential, -wave_x * wave_y * potential, -wave_y * wave_y * potential]
    return jnp.stack([jnp.real(jnp.fft.ifft2(single))[:NG, :NG] for single in spectra]).astype(jnp.float32)

def sample(fields, row_pos, col_pos):
    margin = NG // TILES + 2
    padded = jnp.pad(fields, ((0, 0), (margin, margin), (margin, margin)))
    row_floor = jnp.floor(row_pos)
    col_floor = jnp.floor(col_pos)
    frac_row = row_pos - row_floor
    frac_col = col_pos - col_floor
    row_ids = row_floor.astype(jnp.int32) + margin
    col_ids = col_floor.astype(jnp.int32) + margin
    return padded[:, row_ids, col_ids] * ((1.0 - frac_row) * (1.0 - frac_col)) + padded[:, row_ids, col_ids + 1] * ((1.0 - frac_row) * frac_col) + padded[:, row_ids + 1, col_ids] * (frac_row * (1.0 - frac_col)) + padded[:, row_ids + 1, col_ids + 1] * (frac_row * frac_col)

def update_state(state, values):
    hess_xx = values[2]
    hess_xy = values[3]
    hess_yy = values[4]
    dist_xx = state[2]
    dist_xy = state[3]
    dist_yx = state[4]
    dist_yy = state[5]
    return jnp.stack([state[0] - LENS_WEIGHT * values[0], state[1] - LENS_WEIGHT * values[1], dist_xx - LENS_WEIGHT * (hess_xx * dist_xx + hess_xy * dist_yx), dist_xy - LENS_WEIGHT * (hess_xx * dist_xy + hess_xy * dist_yy), dist_yx - LENS_WEIGHT * (hess_xy * dist_xx + hess_yy * dist_yx), dist_yy - LENS_WEIGHT * (hess_xy * dist_xy + hess_yy * dist_yy)])

def advance(state, fields, base_row, base_col, span):
    row_pos = base_row + span * jnp.tanh(state[0] / span)
    col_pos = base_col + span * jnp.tanh(state[1] / span)
    return update_state(state, sample(fields, row_pos, col_pos))

def reference(block_dest, particle_cell, particle_offset, particle_mass, ray_cell, ray_offset):
    tile_rows = NG // TILES

    def plane_work(inputs):
        return plane_fields(deposit_plane(inputs[0], inputs[1], inputs[2], inputs[3]))
    fields = lax.map(plane_work, (block_dest[:, :, 0], particle_cell, particle_offset, particle_mass))
    tile_of = (jnp.arange(TILES * RAYS, dtype=jnp.int32) // RAYS)[None, :]
    base_row = ((tile_of * tile_rows + ray_cell // NG).astype(jnp.float32) + ray_offset[0]).reshape(-1)
    base_col = ((ray_cell % NG).astype(jnp.float32) + ray_offset[1]).reshape(-1)
    total = base_row.shape[0]
    ones_row = jnp.ones((total,), jnp.float32)
    zeros_row = jnp.zeros((total,), jnp.float32)
    start_state = jnp.stack([zeros_row, zeros_row, ones_row, zeros_row, zeros_row, ones_row])
    span = float(tile_rows - 1)

    def one_plane(state, fields_now):
        moved = advance(state, fields_now, base_row, base_col, span)
        return (moved, moved)
    _, states = lax.scan(one_plane, start_state, fields)
    ray_maps = states.reshape(PLANES, 6, NB, TILES * RAYS).transpose(0, 2, 1, 3)
    return (fields, ray_maps)
```

```python
import math

import jax
import jax.numpy as jnp
import numpy as np
from jax import lax
from jax.experimental import pallas as pl
from jax.experimental.pallas import tpu as pltpu
from jax.sharding import PartitionSpec as P

NG = 512
NP = 2 * NG
HALF = NP // 2
BLOCKS_DEV = 64

LENS_WEIGHT = 0.15
SCREEN_SCALE = 0.5
MU2 = (SCREEN_SCALE * 2.0 * math.pi / NP) ** 2
WAVE = 2.0 * math.pi / NP
F32 = jnp.float32
BF16 = jnp.bfloat16
VMEM = pltpu.VMEM
RAY_CHUNK = 256


def vmem_spec():
    return pl.BlockSpec(memory_space=pltpu.VMEM)


def smem_spec():
    return pl.BlockSpec(memory_space=pltpu.SMEM)


def split(x):
    hi = x.astype(BF16)
    return hi, (x - hi.astype(F32)).astype(BF16)


def dot_nt(a, b):
    return lax.dot_general(a, b, (((1,), (1,)), ((), ())), preferred_element_type=F32)


def dot_nn(a, b):
    return lax.dot_general(a, b, (((1,), (0,)), ((), ())), preferred_element_type=F32)


def route_kernel(dest_ref, cell_ref, offset_ref, mass_ref, out_ref, count_ref):
    tiles = count_ref.shape[0]
    blocks = cell_ref.shape[1]
    cap = out_ref.shape[0] // (4 * tiles)
    out_ref[...] = jnp.zeros(out_ref.shape, F32)
    for t in range(tiles):
        count_ref[t] = 0

    def place(i, carry):
        dest = dest_ref[i]
        rank = count_ref[dest]
        count_ref[dest] = rank + 1
        row = dest * (4 * cap) + rank
        out_ref[pl.ds(row, 1), :] = cell_ref[0, pl.ds(i, 1), :].astype(F32)
        out_ref[pl.ds(row + cap, 1), :] = offset_ref[0, 0, pl.ds(i, 1), :]
        out_ref[pl.ds(row + 2 * cap, 1), :] = offset_ref[0, 1, pl.ds(i, 1), :]
        out_ref[pl.ds(row + 3 * cap, 1), :] = mass_ref[0, pl.ds(i, 1), :]
        return carry

    lax.fori_loop(0, blocks, place, 0)


def deposit_kernel(in_ref, out_ref, acc_ref, *, scaling, tile_rows):
    tiles = in_ref.shape[0]
    cap = in_ref.shape[1] // 4
    lanes = in_ref.shape[2]
    group = min(8, cap)
    rows = -(-(tile_rows + 1) // 16) * 16
    acc_ref[...] = jnp.zeros(acc_ref.shape, F32)
    row_iota = lax.broadcasted_iota(jnp.int32, (rows, lanes), 0).astype(F32).astype(BF16)
    col_iota = (lax.broadcasted_iota(jnp.int32, (NG, lanes), 0) - NG // 2).astype(F32).astype(BF16)
    zero = jnp.zeros((), BF16)
    one = jnp.ones((), BF16)

    def step(src, start):
        pieces_r = []
        pieces_c = []
        for j in range(start, start + group):
            cell = in_ref[src, pl.ds(j, 1), :].astype(jnp.int32)
            frac_r = in_ref[src, pl.ds(cap + j, 1), :]
            frac_c = in_ref[src, pl.ds(2 * cap + j, 1), :]
            mass = in_ref[src, pl.ds(3 * cap + j, 1), :]
            row_id = (cell // NG).astype(F32)
            col_id = (cell % NG - NG // 2).astype(F32).astype(BF16)
            first = row_iota == row_id.astype(BF16)
            second = row_iota == (row_id + 1.0).astype(BF16)
            upper = mass * (1.0 - frac_r)
            lower = mass * frac_r
            rows_now = []
            for side in (1.0 - frac_c, frac_c):
                a_hi, a_lo = split(upper * side)
                b_hi, b_lo = split(lower * side)
                rows_now.append(jnp.where(first, a_hi, jnp.where(second, b_hi, zero)))
                rows_now.append(jnp.where(first, a_lo, jnp.where(second, b_lo, zero)))
            pieces_r.append(jnp.concatenate(rows_now, axis=0))
            pieces_c.append(jnp.where(col_iota == col_id, one, zero))
        acc_ref[...] += dot_nt(jnp.concatenate(pieces_r, axis=1), jnp.concatenate(pieces_c, axis=1))

    def per_source(src, carry):
        step(src, 0)
        for start in range(group, cap, group):
            block = in_ref[src, pl.ds(3 * cap + start, group), :]

            @pl.when(jnp.max(jnp.abs(block)) > 0.0)
            def _():
                step(src, start)

        return carry

    lax.fori_loop(0, tiles, per_source, 0)
    near = acc_ref[0:rows, :] + acc_ref[rows : 2 * rows, :]
    far = acc_ref[2 * rows : 3 * rows, :] + acc_ref[3 * rows : 4 * rows, :]
    lane = lax.broadcasted_iota(jnp.int32, (rows, NG), 1)
    total = (near + jnp.where(lane == 0, 0.0, pltpu.roll(far, 1, 1))) * scaling
    out_ref[...] = total[0 : out_ref.shape[0], :]


def fields_kernel(
    info_ref,
    mine_ref,
    other_ref,
    v_hi_ref,
    v_lo_ref,
    w0_ref,
    phase_ref,
    lens_ref,
    tab_hi_ref,
    tab_lo_ref,
    dens_ref,
    dens_hi_ref,
    dens_lo_ref,
    u_hi_ref,
    u_lo_ref,
    ba_ref,
    l_hi_ref,
    l_lo_ref,
    *,
    tile_rows,
):
    tile = info_ref[0]
    parity = info_ref[1]
    pairs = mine_ref.shape[0]
    tiles = 2 * pairs
    win = 3 * tile_rows
    pad = tile_rows
    zeros = jnp.zeros((pad, NG), F32)
    dens_ref[0:pad, :] = zeros
    dens_ref[pad + NG : pad + NG + pad, :] = zeros
    for half, src in ((0, mine_ref), (1, other_ref)):
        for j in range(pairs):
            t = 2 * j + jnp.bitwise_xor(parity, half)
            row = pl.multiple_of(pad + t * tile_rows, 8)
            dens_ref[pl.ds(row, tile_rows), :] = src[j, 0:tile_rows, :]
    for half, src in ((0, mine_ref), (1, other_ref)):
        for j in range(pairs):
            t = 2 * j + jnp.bitwise_xor(parity, half)
            row = pl.multiple_of(pad + (t + 1) * tile_rows, 8)
            spill = jnp.where(t + 1 < tiles, src[j, tile_rows : tile_rows + 8, :], 0.0)
            dens_ref[pl.ds(row, 8), :] += spill
    d_hi, d_lo = split(dens_ref[pad : pad + NG, :])
    dens_hi_ref[...] = d_hi
    dens_lo_ref[...] = d_lo

    half_lane = lax.broadcasted_iota(jnp.int32, (1, HALF), 1).astype(F32) * WAVE
    w_cos = w0_ref[:, 0:HALF]
    w_sin = w0_ref[:, HALF:NP]
    for rows, cols, value in (
        (0, 0, w_cos),
        (0, HALF, w_sin),
        (win, 0, -half_lane * w_sin),
        (win, HALF, half_lane * w_cos),
    ):
        hi, lo = split(value)
        u_hi_ref[rows : rows + win, cols : cols + HALF] = hi
        u_lo_ref[rows : rows + win, cols : cols + HALF] = lo

    lane = lax.broadcasted_iota(jnp.int32, (1, NP), 1)
    k_slot = jnp.where(lane < HALF, lane, jnp.where(lane == HALF, HALF, lane - HALF))
    kx = k_slot.astype(F32) * WAVE
    kx2 = kx * kx
    edge_k = (lane == 0) | (lane == HALF)
    weight_k = jnp.where(edge_k, 1.0, 2.0)
    block = 256
    turn_cos = phase_ref[0:1, :]
    turn_sin = phase_ref[1:2, :]

    def channel_block(i, corner):
        at = pl.multiple_of(i * block, block)
        v_hi = v_hi_ref[pl.ds(at, block), :]
        v_lo = v_lo_ref[pl.ds(at, block), :]
        dh = dens_hi_ref[...]
        first = dot_nt(v_hi, dh) + dot_nt(v_lo, dh) + dot_nt(v_hi, dens_lo_ref[...])
        f_hi, f_lo = split(first)
        spec = (
            dot_nt(f_hi, v_hi_ref[...]) + dot_nt(f_lo, v_hi_ref[...]) + dot_nt(f_hi, v_lo_ref[...])
        )
        chan = at + lax.broadcasted_iota(jnp.int32, (block, 1), 0)
        l_slot = jnp.where(chan < HALF, chan, jnp.where(chan == HALF, HALF, chan - HALF))
        ky = l_slot.astype(F32) * WAVE
        weight_l = jnp.where((chan == 0) | (chan == HALF), 1.0, 2.0)
        scale = (weight_l * (-2.0 / (NP * NP))) * weight_k
        pot = spec * (scale / (kx2 + ky * ky + MU2))
        corner = jnp.where(i == HALF // block, pot[0:1, HALF : HALF + 1], corner)
        pot_c = pot[:, 0:HALF]
        pot_s = pot[:, HALF:NP]
        turned = jnp.concatenate(
            [pot_c * turn_cos + pot_s * turn_sin, pot_s * turn_cos - pot_c * turn_sin], axis=1
        )
        p_hi, p_lo = split(turned)
        uh = u_hi_ref[...]
        ba_ref[:, pl.ds(at, block)] = (
            dot_nt(uh, p_hi) + dot_nt(u_lo_ref[...], p_hi) + dot_nt(uh, p_lo)
        )
        return corner

    corner = lax.fori_loop(0, NP // block, channel_block, jnp.zeros((1, 1), F32))

    row_at = lax.broadcasted_iota(jnp.int32, (win, 1), 0)
    grid_row = (tile - 1) * tile_rows + row_at
    inside = ((grid_row >= 0) & (grid_row < NG)).astype(F32)
    b_all = ba_ref[0:win, :] * inside
    a_all = ba_ref[win : 2 * win, :] * inside
    ky2 = kx2
    sign = (1 - 2 * (row_at % 2)).astype(F32)
    corner_col = inside * sign * corner * (-math.pi * math.pi)
    lane_half = lax.broadcasted_iota(jnp.int32, (1, HALF), 1)

    def store(field, value):
        hi, lo = split(value)
        l_hi_ref[field] = hi
        l_lo_ref[field] = lo

    store(0, a_all)
    store(
        1,
        jnp.concatenate([half_lane * b_all[:, HALF:NP], -half_lane * b_all[:, 0:HALF]], axis=1),
    )
    store(2, (MU2 + ky2) * b_all)
    store(
        3,
        jnp.concatenate(
            [
                half_lane * a_all[:, HALF:NP],
                jnp.where(lane_half == 0, corner_col, -half_lane * a_all[:, 0:HALF]),
            ],
            axis=1,
        ),
    )
    store(4, -ky2 * b_all)

    def one_field(f, carry):
        lh = l_hi_ref[f]
        vh = v_hi_ref[...]
        out = dot_nn(lh, vh) + dot_nn(l_lo_ref[f], vh) + dot_nn(lh, v_lo_ref[...])
        row = pl.multiple_of(tile * tile_rows, 8)
        out = out + jnp.where(f == 2, 2.0, 0.0) * dens_ref[pl.ds(row, win), :]
        lens_ref[0, f] = out[tile_rows : 2 * tile_rows, :]
        hi, lo = split(out)
        tab_hi_ref[f] = hi
        tab_lo_ref[f] = lo
        return carry

    lax.fori_loop(0, 5, one_field, 0)


def ray_kernel(info_ref, inbox_ref, cell_ref, offset_ref, tab_hi_ref, tab_lo_ref, out_ref, *, tile_rows):
    batch = info_ref[0]
    first_plane = info_ref[1]
    tile = info_ref[2]
    active = info_ref[3]
    rays = out_ref.shape[1]
    fields, win, _ = tab_hi_ref.shape
    span = float(tile_rows - 1)
    n = RAY_CHUNK
    col_iota = (lax.broadcasted_iota(jnp.int32, (NG, n), 0) - NG // 2).astype(F32).astype(BF16)
    row_iota = lax.broadcasted_iota(jnp.int32, (win, n), 0)
    unit_row = lax.broadcasted_iota(jnp.int32, (6, n), 0)
    unit = jnp.where((unit_row == 2) | (unit_row == 5), 1.0, 0.0)
    zero = jnp.zeros((), BF16)

    def chunk(i, carry):
        at = pl.multiple_of(i * n, n)
        state = jnp.where(first_plane > 0, unit, inbox_ref[:, pl.ds(at, n)])
        cell = cell_ref[pl.ds(batch, 1), pl.ds(at, n)]
        base_row = (tile * tile_rows + cell // NG).astype(F32) + offset_ref[0, pl.ds(batch, 1), pl.ds(at, n)]
        base_col = (cell % NG).astype(F32) + offset_ref[1, pl.ds(batch, 1), pl.ds(at, n)]
        dx = state[0:1]
        dy = state[1:2]
        row_pos = base_row + span * jnp.tanh(dx / span)
        col_pos = base_col + span * jnp.tanh(dy / span)
        row_floor = jnp.floor(row_pos)
        col_floor = jnp.floor(col_pos)
        frac_row = row_pos - row_floor
        frac_col = col_pos - col_floor
        row_id = row_floor.astype(jnp.int32) - (tile - 1) * tile_rows
        row_w = jnp.where(row_iota == row_id, 1.0 - frac_row, 0.0) + jnp.where(
            row_iota == row_id + 1, frac_row, 0.0
        )
        far = 4.0 * NG
        c0 = jnp.where((col_floor >= 0.0) & (col_floor < NG), col_floor - NG // 2, far).astype(BF16)
        c1 = jnp.where(
            (col_floor >= -1.0) & (col_floor < NG - 1.0), col_floor + (1.0 - NG // 2), far
        ).astype(BF16)
        g0_hi, g0_lo = split(1.0 - frac_col)
        g1_hi, g1_lo = split(frac_col)
        here = col_iota == c0
        there = col_iota == c1
        w_hi = jnp.where(here, g0_hi, jnp.where(there, g1_hi, zero))
        w_lo = jnp.where(here, g0_lo, jnp.where(there, g1_lo, zero))
        values = []
        for f in range(fields):
            th = tab_hi_ref[f]
            along = dot_nn(th, w_hi) + dot_nn(tab_lo_ref[f], w_hi) + dot_nn(th, w_lo)
            values.append(jnp.sum(along * row_w, axis=0, keepdims=True))
        ax, ay, hxx, hxy, hyy = values
        a11 = state[2:3]
        a12 = state[3:4]
        a21 = state[4:5]
        a22 = state[5:6]
        out_ref[:, pl.ds(at, n)] = jnp.concatenate(
            [
                dx - LENS_WEIGHT * ax,
                dy - LENS_WEIGHT * ay,
                a11 - LENS_WEIGHT * (hxx * a11 + hxy * a21),
                a12 - LENS_WEIGHT * (hxx * a12 + hxy * a22),
                a21 - LENS_WEIGHT * (hxy * a11 + hyy * a21),
                a22 - LENS_WEIGHT * (hxy * a12 + hyy * a22),
            ],
            axis=0,
        )
        return carry

    @pl.when(active > 0)
    def _():
        lax.fori_loop(0, rays // n, chunk, 0)

    @pl.when(active == 0)
    def _():
        out_ref[...] = jnp.zeros(out_ref.shape, F32)


def trig_table(rows):
    m = np.arange(rows)[:, None]
    k = np.arange(HALF)[None, :]
    phase = (m * k % NP) * (2.0 * np.pi / NP)
    table = np.concatenate([np.cos(phase), np.sin(phase)], axis=1)
    table[:, HALF] = 1.0 - 2.0 * (np.arange(rows) % 2)
    return table


def per_device(block_dest, particle_cell, particle_offset, particle_mass, ray_cell, ray_offset):
    tiles = lax.axis_size("tile")
    planes = lax.axis_size("plane")
    tile_rows = NG // tiles
    tile_now = lax.axis_index("tile")
    plane_now = lax.axis_index("plane")
    blocks = particle_cell.shape[1]
    block_len = particle_cell.shape[2]
    cap = 2 * blocks // tiles
    win = 3 * tile_rows

    outgoing = pl.pallas_call(
        route_kernel,
        out_shape=jax.ShapeDtypeStruct((tiles * 4 * cap, block_len), F32),
        in_specs=[smem_spec(), vmem_spec(), vmem_spec(), vmem_spec()],
        out_specs=vmem_spec(),
        scratch_shapes=[pltpu.SMEM((tiles,), jnp.int32)],
        name="route",
    )(block_dest.reshape(-1), particle_cell, particle_offset, particle_mass)
    incoming = lax.all_to_all(
        outgoing.reshape(tiles, 4 * cap, block_len), "tile", split_axis=0, concat_axis=0, tiled=True
    )

    scaling = math.sqrt(tile_rows * NG / (BLOCKS_DEV * block_len))
    rows_acc = -(-(tile_rows + 1) // 16) * 16
    canvas_rows = tile_rows + 8
    canvas = pl.pallas_call(
        lambda a, b, c: deposit_kernel(a, b, c, scaling=scaling, tile_rows=tile_rows),
        out_shape=jax.ShapeDtypeStruct((canvas_rows, NG), F32),
        in_specs=[vmem_spec()],
        out_specs=vmem_spec(),
        scratch_shapes=[VMEM((4 * rows_acc, NG), F32)],
        name="deposit",
    )(incoming)

    groups = [[i for i in range(tiles) if i % 2 == p] for p in (0, 1)]
    mine = lax.all_gather(canvas, "tile", axis=0, tiled=False, axis_index_groups=groups)
    other = lax.ppermute(mine, "tile", [(i, i ^ 1) for i in range(tiles)])

    v = trig_table(NG).T.astype(np.float32)
    v_hi = v.astype(jnp.bfloat16)
    v_lo = (v - v_hi.astype(np.float32)).astype(jnp.bfloat16)
    w0 = trig_table(win).astype(np.float32)
    k_index = lax.broadcasted_iota(jnp.int32, (1, HALF), 1)
    origin = (tile_now - 1) * tile_rows + NP
    turn = (k_index * origin % NP).astype(F32) * WAVE
    phase = jnp.concatenate([jnp.cos(turn), jnp.sin(turn)], axis=0)
    info = jnp.stack([tile_now, tile_now % 2]).astype(jnp.int32)
    lens, tab_hi, tab_lo = pl.pallas_call(
        lambda *refs: fields_kernel(*refs, tile_rows=tile_rows),
        out_shape=(
            jax.ShapeDtypeStruct((1, 5, tile_rows, NG), F32),
            jax.ShapeDtypeStruct((5, win, NG), BF16),
            jax.ShapeDtypeStruct((5, win, NG), BF16),
        ),
        in_specs=[smem_spec()] + [vmem_spec()] * 6,
        out_specs=(vmem_spec(), vmem_spec(), vmem_spec()),
        scratch_shapes=[
            VMEM((NG + 2 * tile_rows, NG), F32),
            VMEM((NG, NG), BF16),
            VMEM((NG, NG), BF16),
            VMEM((2 * win, NP), BF16),
            VMEM((2 * win, NP), BF16),
            VMEM((2 * win, NP), F32),
            VMEM((5, win, NP), BF16),
            VMEM((5, win, NP), BF16),
        ],
        name="fields",
    )(info, mine, other, jnp.asarray(v_hi), jnp.asarray(v_lo), jnp.asarray(w0), phase)

    batches = ray_cell.shape[0]
    rays = ray_cell.shape[1]
    ring = [(i, (i + 1) % planes) for i in range(planes)]
    inbox = jnp.zeros((6, rays), F32)
    states = []
    for turn_index in range(batches + planes - 1):
        batch = turn_index - plane_now
        active = (batch >= 0) & (batch < batches)
        ray_info = jnp.stack(
            [
                jnp.clip(batch, 0, batches - 1),
                (plane_now == 0).astype(jnp.int32),
                tile_now,
                active.astype(jnp.int32),
            ]
        ).astype(jnp.int32)
        moved = pl.pallas_call(
            lambda *refs: ray_kernel(*refs, tile_rows=tile_rows),
            out_shape=jax.ShapeDtypeStruct((6, rays), F32),
            in_specs=[smem_spec()] + [vmem_spec()] * 5,
            out_specs=vmem_spec(),
            name="rays",
        )(ray_info, inbox, ray_cell, ray_offset, tab_hi, tab_lo)
        states.append(moved)
        if turn_index < batches + planes - 2:
            inbox = lax.ppermute(moved, "plane", ring)
    ray_maps = lax.dynamic_slice_in_dim(jnp.stack(states), plane_now, batches, axis=0)
    return (lens, ray_maps[None])


def solution(mesh):
    return jax.shard_map(
        per_device,
        mesh=mesh,
        in_specs=(
            P("plane", "tile", None),
            P("plane", "tile", None),
            P("plane", None, "tile", None),
            P("plane", "tile", None),
            P(None, "tile"),
            P(None, None, "tile"),
        ),
        out_specs=(P("plane", None, "tile", None), P("plane", None, None, "tile")),
        check_vma=False,
    )
```

```python
import math

import jax
import jax.numpy as jnp
from jax import lax
from jax.experimental import pallas as pl
from jax.experimental.pallas import tpu as pltpu
from jax.sharding import PartitionSpec as P

NG = 512
NP = 2 * NG
HALF = NP // 2
BLOCKS_DEV = 64

LENS_WEIGHT = 0.15
SCREEN_SCALE = 0.5
MU2 = (SCREEN_SCALE * 2.0 * math.pi / NP) ** 2
WAVE = 2.0 * math.pi / NP
F32 = jnp.float32
BF16 = jnp.bfloat16
VMEM = pltpu.VMEM
RAY_CHUNK = 512
GROUP = 2
SUB = 16
TIERS = (5, 6, 7)


def vmem_spec():
    return pl.BlockSpec(memory_space=pltpu.VMEM)


def hbm_spec():
    return pl.BlockSpec(memory_space=pltpu.HBM)


def params(mib):
    return pltpu.CompilerParams(vmem_limit_bytes=mib * 1024 * 1024)


def smem_spec():
    return pl.BlockSpec(memory_space=pltpu.SMEM)


def split(x):
    hi = x.astype(BF16)
    return hi, (x - hi.astype(F32)).astype(BF16)


def dot_nt(a, b):
    return lax.dot_general(a, b, (((1,), (1,)), ((), ())), preferred_element_type=F32)


def dot_nn(a, b):
    return lax.dot_general(a, b, (((1,), (0,)), ((), ())), preferred_element_type=F32)


def route_kernel(dest_hbm, cell_hbm, offset_hbm, mass_hbm, out_ref, dest_ref, cell_ref, offset_ref, mass_ref, count_ref, sems):
    copies = [
        pltpu.make_async_copy(src, dst, sems.at[i])
        for i, (src, dst) in enumerate(
            (
                (dest_hbm, dest_ref),
                (cell_hbm, cell_ref),
                (offset_hbm, offset_ref),
                (mass_hbm, mass_ref),
            )
        )
    ]
    for copy in copies:
        copy.start()
    tiles = count_ref.shape[0]
    blocks = cell_ref.shape[1]
    cap = out_ref.shape[0] // (4 * tiles)
    out_ref[...] = jnp.zeros(out_ref.shape, F32)
    for t in range(tiles):
        count_ref[t] = 0
    for copy in copies:
        copy.wait()

    def place(i, carry):
        dest = dest_ref[i]
        rank = count_ref[dest]
        count_ref[dest] = rank + 1
        row = dest * (4 * cap) + rank
        out_ref[pl.ds(row, 1), :] = cell_ref[0, pl.ds(i, 1), :].astype(F32)
        out_ref[pl.ds(row + cap, 1), :] = offset_ref[0, 0, pl.ds(i, 1), :]
        out_ref[pl.ds(row + 2 * cap, 1), :] = offset_ref[0, 1, pl.ds(i, 1), :]
        out_ref[pl.ds(row + 3 * cap, 1), :] = mass_ref[0, pl.ds(i, 1), :]
        return carry

    lax.fori_loop(0, blocks, place, 0)


def deposit_kernel(in_ref, out_ref, acc_ref, *, scaling, tile_rows):
    tiles = in_ref.shape[0]
    cap = in_ref.shape[1] // 4
    lanes = in_ref.shape[2]
    group = min(8, cap)
    rows = -(-(tile_rows + 1) // 16) * 16
    acc_ref[...] = jnp.zeros(acc_ref.shape, F32)
    row_iota = lax.broadcasted_iota(jnp.int32, (rows, lanes), 0).astype(F32).astype(BF16)
    col_iota = (lax.broadcasted_iota(jnp.int32, (NG, lanes), 0) - NG // 2).astype(F32).astype(BF16)
    zero = jnp.zeros((), BF16)
    one = jnp.ones((), BF16)

    def step(src, start):
        pieces_r = []
        pieces_c = []
        for j in range(start, start + group):
            cell = in_ref[src, pl.ds(j, 1), :].astype(jnp.int32)
            frac_r = in_ref[src, pl.ds(cap + j, 1), :]
            frac_c = in_ref[src, pl.ds(2 * cap + j, 1), :]
            mass = in_ref[src, pl.ds(3 * cap + j, 1), :]
            row_id = (cell // NG).astype(F32)
            col_id = (cell % NG - NG // 2).astype(F32).astype(BF16)
            first = row_iota == row_id.astype(BF16)
            second = row_iota == (row_id + 1.0).astype(BF16)
            upper = mass * (1.0 - frac_r)
            lower = mass * frac_r
            rows_now = []
            for side in (1.0 - frac_c, frac_c):
                a_hi, a_lo = split(upper * side)
                b_hi, b_lo = split(lower * side)
                rows_now.append(jnp.where(first, a_hi, jnp.where(second, b_hi, zero)))
                rows_now.append(jnp.where(first, a_lo, jnp.where(second, b_lo, zero)))
            pieces_r.append(jnp.concatenate(rows_now, axis=0))
            pieces_c.append(jnp.where(col_iota == col_id, one, zero))
        acc_ref[...] += dot_nt(jnp.concatenate(pieces_r, axis=1), jnp.concatenate(pieces_c, axis=1))

    def per_source(src, carry):
        step(src, 0)
        for start in range(group, cap, group):
            block = in_ref[src, pl.ds(3 * cap + start, group), :]

            @pl.when(jnp.max(jnp.abs(block)) > 0.0)
            def _():
                step(src, start)

        return carry

    lax.fori_loop(0, tiles, per_source, 0)
    near = acc_ref[0:rows, :] + acc_ref[rows : 2 * rows, :]
    far = acc_ref[2 * rows : 3 * rows, :] + acc_ref[3 * rows : 4 * rows, :]
    lane = lax.broadcasted_iota(jnp.int32, (rows, NG), 1)
    total = (near + jnp.where(lane == 0, 0.0, pltpu.roll(far, 1, 1))) * scaling
    out_ref[...] = total[0 : out_ref.shape[0], :]


def unit_circle(left, right):
    turn = (left * right % NP).astype(F32) * WAVE
    return jnp.cos(turn), jnp.sin(turn)


def tables_kernel(v_hi_ref, v_lo_ref, u_hi_ref, u_lo_ref):
    lanes = 128
    fine = 32
    shape = (HALF // fine, lanes)
    coarse_c, coarse_s = unit_circle(
        fine * lax.broadcasted_iota(jnp.int32, shape, 0), lax.broadcasted_iota(jnp.int32, shape, 1)
    )
    shape = (fine, lanes)
    fine_c, fine_s = unit_circle(
        lax.broadcasted_iota(jnp.int32, shape, 0), lax.broadcasted_iota(jnp.int32, shape, 1)
    )
    parity = (1 - 2 * (lax.broadcasted_iota(jnp.int32, shape, 1) % 2)).astype(F32)
    first = lax.broadcasted_iota(jnp.int32, shape, 0) == 0
    for a in range(HALF // fine):
        ca = coarse_c[a : a + 1, :]
        sa = coarse_s[a : a + 1, :]
        base_cos = fine_c * ca - fine_s * sa
        base_sin = fine_s * ca + fine_c * sa
        k_index = a * fine + lax.broadcasted_iota(jnp.int32, shape, 0)
        for j in range(NG // lanes):
            q_cos, q_sin = 1.0, 0.0
            if j:
                step = NP // math.gcd(NP, lanes * j)
                turn = (k_index * (lanes * j)) % NP
                q_cos = jnp.ones(shape, F32)
                q_sin = jnp.zeros(shape, F32)
                for q in range(1, step):
                    angle = 2.0 * math.pi * q / step
                    hit = turn == q * (NP // step)
                    q_cos = jnp.where(hit, math.cos(angle), q_cos)
                    q_sin = jnp.where(hit, math.sin(angle), q_sin)
            cos_now = base_cos * q_cos - base_sin * q_sin
            sin_now = base_sin * q_cos + base_cos * q_sin
            if a == 0:
                sin_now = jnp.where(first, parity, sin_now)
            for at, value in ((0, cos_now), (HALF, sin_now)):
                hi, lo = split(value)
                v_hi_ref[at + a * fine : at + (a + 1) * fine, j * lanes : (j + 1) * lanes] = hi
                v_lo_ref[at + a * fine : at + (a + 1) * fine, j * lanes : (j + 1) * lanes] = lo
    win = u_hi_ref.shape[0] // 2
    fine = 16
    shape = (fine, HALF)
    fine_c, fine_s = unit_circle(
        lax.broadcasted_iota(jnp.int32, shape, 0), lax.broadcasted_iota(jnp.int32, shape, 1)
    )
    lane = lax.broadcasted_iota(jnp.int32, shape, 1)
    wave = lane.astype(F32) * WAVE
    parity = (1 - 2 * (lax.broadcasted_iota(jnp.int32, shape, 0) % 2)).astype(F32)
    for a in range(win // fine):
        ca, sa = unit_circle(jnp.full((1, HALF), a * fine, jnp.int32), lane[0:1])
        w_cos = fine_c * ca - fine_s * sa
        w_sin = fine_s * ca + fine_c * sa
        for rows, cols, value in (
            (0, 0, w_cos),
            (0, HALF, jnp.where(lane == 0, parity, w_sin)),
            (win, 0, -wave * w_sin),
            (win, HALF, wave * w_cos),
        ):
            hi, lo = split(value)
            u_hi_ref[rows + a * fine : rows + (a + 1) * fine, cols : cols + HALF] = hi
            u_lo_ref[rows + a * fine : rows + (a + 1) * fine, cols : cols + HALF] = lo


def fields_kernel(
    mine_ref,
    other_ref,
    v_hi_ref,
    v_lo_ref,
    u_hi_ref,
    u_lo_ref,
    lens_ref,
    tab_ref,
    ba_ref,
    window_ref,
    corner_ref,
    dens_ref,
    dens_hi_ref,
    dens_lo_ref,
    l_hi_ref,
    l_lo_ref,
    *,
    tile_rows,
):
    tile = lax.axis_index("tile")
    parity = tile % 2
    pairs = mine_ref.shape[0]
    tiles = 2 * pairs
    win = 3 * tile_rows
    pad = tile_rows
    zeros = jnp.zeros((pad, NG), F32)
    dens_ref[0:pad, :] = zeros
    dens_ref[pad + NG : pad + NG + pad, :] = zeros
    for half, src in ((0, mine_ref), (1, other_ref)):
        for j in range(pairs):
            t = 2 * j + jnp.bitwise_xor(parity, half)
            row = pl.multiple_of(pad + t * tile_rows, 8)
            dens_ref[pl.ds(row, tile_rows), :] = src[j, 0:tile_rows, :]
    for half, src in ((0, mine_ref), (1, other_ref)):
        for j in range(pairs):
            t = 2 * j + jnp.bitwise_xor(parity, half)
            row = pl.multiple_of(pad + (t + 1) * tile_rows, 8)
            spill = jnp.where(t + 1 < tiles, src[j, tile_rows : tile_rows + 8, :], 0.0)
            dens_ref[pl.ds(row, 8), :] += spill
    d_hi, d_lo = split(dens_ref[pad : pad + NG, :])
    dens_hi_ref[...] = d_hi
    dens_lo_ref[...] = d_lo

    half_lane = lax.broadcasted_iota(jnp.int32, (1, HALF), 1).astype(F32) * WAVE
    origin = (tile - 1) * tile_rows + NP
    turn = (lax.broadcasted_iota(jnp.int32, (1, HALF), 1) * origin % NP).astype(F32) * WAVE
    turn_cos = jnp.cos(turn)
    turn_sin = jnp.sin(turn)
    lane = lax.broadcasted_iota(jnp.int32, (1, NP), 1)
    k_slot = jnp.where(lane < HALF, lane, jnp.where(lane == HALF, HALF, lane - HALF))
    kx = k_slot.astype(F32) * WAVE
    kx2 = kx * kx
    edge_k = (lane == 0) | (lane == HALF)
    weight_k = jnp.where(edge_k, 1.0, 2.0)
    block = 256

    def channel_block(i, corner):
        at = pl.multiple_of(i * block, block)
        v_hi = v_hi_ref[pl.ds(at, block), :]
        v_lo = v_lo_ref[pl.ds(at, block), :]
        dh = dens_hi_ref[...]
        first = dot_nt(v_hi, dh) + dot_nt(v_lo, dh) + dot_nt(v_hi, dens_lo_ref[...])
        f_hi, f_lo = split(first)
        spec = (
            dot_nt(f_hi, v_hi_ref[...]) + dot_nt(f_lo, v_hi_ref[...]) + dot_nt(f_hi, v_lo_ref[...])
        )
        chan = at + lax.broadcasted_iota(jnp.int32, (block, 1), 0)
        l_slot = jnp.where(chan < HALF, chan, jnp.where(chan == HALF, HALF, chan - HALF))
        ky = l_slot.astype(F32) * WAVE
        weight_l = jnp.where((chan == 0) | (chan == HALF), 1.0, 2.0)
        scale = (weight_l * (-2.0 / (NP * NP))) * weight_k
        pot = spec * (scale / (kx2 + ky * ky + MU2))
        corner = jnp.where(i == HALF // block, pot[0:1, HALF : HALF + 1], corner)
        pot_c = pot[:, 0:HALF]
        pot_s = pot[:, HALF:NP]
        turned = jnp.concatenate(
            [pot_c * turn_cos + pot_s * turn_sin, pot_s * turn_cos - pot_c * turn_sin], axis=1
        )
        p_hi, p_lo = split(turned)
        uh = u_hi_ref[...]
        ba_ref[:, pl.ds(at, block)] = (
            dot_nt(uh, p_hi) + dot_nt(u_lo_ref[...], p_hi) + dot_nt(uh, p_lo)
        )
        return corner

    corner = lax.fori_loop(0, NP // block, channel_block, jnp.zeros((1, 1), F32))

    row_at = lax.broadcasted_iota(jnp.int32, (win, 1), 0)
    grid_row = (tile - 1) * tile_rows + row_at
    inside = ((grid_row >= 0) & (grid_row < NG)).astype(F32)
    b_all = ba_ref[0:win, :] * inside
    a_all = ba_ref[win : 2 * win, :] * inside
    ba_ref[0:win, :] = b_all
    ba_ref[win : 2 * win, :] = a_all
    window_ref[...] = dens_ref[pl.ds(pl.multiple_of(tile * tile_rows, 8), win), :]
    corner_ref[...] = jnp.broadcast_to(corner * (-math.pi * math.pi), corner_ref.shape)
    slope = jnp.concatenate([half_lane * b_all[:, HALF:NP], -half_lane * b_all[:, 0:HALF]], axis=1)
    for f, value in enumerate((a_all, slope)):
        hi, lo = split(value)
        l_hi_ref[f * win : (f + 1) * win, :] = hi
        l_lo_ref[f * win : (f + 1) * win, :] = lo
    finish(2, l_hi_ref, l_lo_ref, v_hi_ref, v_lo_ref, None, lens_ref, tab_ref, tile_rows)


def finish(count, l_hi_ref, l_lo_ref, v_hi_ref, v_lo_ref, extra_ref, lens_ref, tab_ref, tile_rows):
    win = 3 * tile_rows
    shape = (win // SUB, SUB, NG)
    vh = v_hi_ref[...]
    out = dot_nn(l_hi_ref[...], vh) + dot_nn(l_lo_ref[...], vh) + dot_nn(l_hi_ref[...], v_lo_ref[...])
    at = lens_ref.shape[-3] - count
    for f in range(count):
        value = out[f * win : (f + 1) * win, :]
        if f == 0 and extra_ref is not None:
            value = value + 2.0 * extra_ref[...]
        lens_ref[..., at + f, :, :] = value[tile_rows : 2 * tile_rows, :].reshape(
            (1,) * (len(lens_ref.shape) - 3) + (tile_rows, NG)
        )
        hi, lo = split(value)
        tab_ref[:, f, :, 0:NG] = hi.reshape(shape)
        tab_ref[:, f, :, NG : 2 * NG] = lo.reshape(shape)
        tab_ref[:, f, :, 2 * NG : 3 * NG] = hi.reshape(shape)


def second_kernel(
    ba_ref,
    window_ref,
    corner_ref,
    part_ref,
    v_hi_ref,
    v_lo_ref,
    lens_ref,
    tab_ref,
    l_hi_ref,
    l_lo_ref,
    *,
    tile_rows,
):
    tile = lax.axis_index("tile")
    win = 3 * tile_rows
    lens_ref[0, 0:2] = part_ref[...]
    row_at = lax.broadcasted_iota(jnp.int32, (win, 1), 0)
    grid_row = (tile - 1) * tile_rows + row_at
    inside = ((grid_row >= 0) & (grid_row < NG)).astype(F32)
    corner_col = inside * (1 - 2 * (row_at % 2)).astype(F32) * corner_ref[0:1, 0:1]
    lane = lax.broadcasted_iota(jnp.int32, (1, NP), 1)
    slot = jnp.where(lane < HALF, lane, jnp.where(lane == HALF, HALF, lane - HALF))
    ky2 = (slot.astype(F32) * WAVE) * (slot.astype(F32) * WAVE)
    lane_half = lax.broadcasted_iota(jnp.int32, (1, HALF), 1)
    half_lane = lane_half.astype(F32) * WAVE
    b_all = ba_ref[0:win, :]
    a_cos = ba_ref[win : 2 * win, 0:HALF]
    a_sin = ba_ref[win : 2 * win, HALF:NP]
    mixed = jnp.concatenate(
        [half_lane * a_sin, jnp.where(lane_half == 0, corner_col, -half_lane * a_cos)], axis=1
    )
    for f, value in enumerate(((MU2 + ky2) * b_all, mixed, -ky2 * b_all)):
        hi, lo = split(value)
        l_hi_ref[f * win : (f + 1) * win, :] = hi
        l_lo_ref[f * win : (f + 1) * win, :] = lo
    finish(3, l_hi_ref, l_lo_ref, v_hi_ref, v_lo_ref, window_ref, lens_ref, tab_ref, tile_rows)


def lookup(geo_ref, tab_ref, emit):
    chunks, fields, _, _ = tab_ref.shape
    group = geo_ref.shape[0] // 4
    rays = geo_ref.shape[1]
    n = min(RAY_CHUNK, rays)
    per = rays // n
    zero = jnp.zeros((), BF16)
    win = chunks * SUB
    least = float(win)
    most = 0.0
    for g in range(group):
        row_id = geo_ref[4 * g : 4 * g + 1, :]
        least = jnp.minimum(least, jnp.min(row_id))
        most = jnp.maximum(most, jnp.max(row_id))
    low = jnp.clip(least.astype(jnp.int32), 0, win - 1) // SUB
    high = jnp.clip(most.astype(jnp.int32) + 1, 0, win - 1) // SUB
    needed = high - low + 1
    tiers = sorted({min(t, chunks) for t in TIERS})

    def with_tier(tier, passes):
        col_iota = (lax.broadcasted_iota(jnp.int32, (NG, n), 0) - NG // 2).astype(F32).astype(BF16)
        row_iota = lax.broadcasted_iota(jnp.int32, (tier * SUB, n), 0).astype(F32)

        def chunk(i, carry):
            g = i // per
            at = pl.multiple_of((i % per) * n, n)
            row_id = geo_ref[pl.ds(4 * g, 1), pl.ds(at, n)]
            frac_row = geo_ref[pl.ds(4 * g + 1, 1), pl.ds(at, n)]
            col_floor = geo_ref[pl.ds(4 * g + 2, 1), pl.ds(at, n)]
            frac_col = geo_ref[pl.ds(4 * g + 3, 1), pl.ds(at, n)]
            far = 4.0 * NG
            c0 = jnp.where((col_floor >= 0.0) & (col_floor < NG), col_floor - NG // 2, far)
            c1 = jnp.where(
                (col_floor >= -1.0) & (col_floor < NG - 1.0), col_floor + (1.0 - NG // 2), far
            )
            here = col_iota == c0.astype(BF16)
            there = col_iota == c1.astype(BF16)
            g0_hi, g0_lo = split(1.0 - frac_col)
            g1_hi, g1_lo = split(frac_col)
            w_hi = jnp.where(here, g0_hi, jnp.where(there, g1_hi, zero))
            w_lo = jnp.where(here, g0_lo, jnp.where(there, g1_lo, zero))
            w = jnp.concatenate([w_hi, w_hi, w_lo], axis=0)

            def rows_from(start, floor):
                here_row = row_id - (start * SUB).astype(F32)
                row_w = jnp.where(row_iota == here_row, 1.0 - frac_row, 0.0) + jnp.where(
                    row_iota == here_row + 1.0, frac_row, 0.0
                )
                if floor is not None:
                    row_w = jnp.where(row_iota >= floor, row_w, 0.0)
                table = tab_ref[pl.ds(start, tier)].reshape(tier * fields * SUB, 3 * NG)
                along = dot_nn(table, w).reshape(tier, fields, SUB, n)
                values = jnp.sum(along * row_w.reshape(tier, 1, SUB, n), axis=0)
                return jnp.sum(values, axis=1)

            if passes == 1:
                values = rows_from(jnp.minimum(low, chunks - tier), None)
            else:

                def one_pass(q, total):
                    start = jnp.minimum(q * tier, chunks - tier)
                    return total + rows_from(start, ((q * tier - start) * SUB).astype(F32))

                values = lax.fori_loop(0, passes, one_pass, jnp.zeros((fields, n), F32))
            emit(g, at, n, values)
            return carry

        lax.fori_loop(0, group * per, chunk, 0)

    floor = 0
    for tier in tiers:
        pl.when((needed > floor) & (needed <= tier))(lambda tier=tier: with_tier(tier, 1))
        floor = tier
    if floor < chunks:
        pl.when(needed > floor)(lambda: with_tier(4, -(-chunks // 4)))


def bent(plane, inbox_a, hess):
    rows = []
    for i in range(hess.shape[0] // 3):
        hxx = hess[3 * i : 3 * i + 1]
        hxy = hess[3 * i + 1 : 3 * i + 2]
        hyy = hess[3 * i + 2 : 3 * i + 3]
        first = plane == 0
        a11, a12, a21, a22 = (
            jnp.where(first, start, inbox_a[4 * i + c : 4 * i + c + 1])
            for c, start in enumerate((1.0, 0.0, 0.0, 1.0))
        )
        rows += [
            a11 - LENS_WEIGHT * (hxx * a11 + hxy * a21),
            a12 - LENS_WEIGHT * (hxx * a12 + hxy * a22),
            a21 - LENS_WEIGHT * (hxy * a11 + hyy * a21),
            a22 - LENS_WEIGHT * (hxy * a12 + hyy * a22),
        ]
    return jnp.concatenate(rows, axis=0)


def move_kernel(*refs, tile_rows, turn):
    if turn:
        inbox_ref, inbox_a_ref, hess_ref, cell_ref, offset_ref, tab_ref, out_ref, bend_ref, geo_ref = refs
    else:
        cell_ref, offset_ref, tab_ref, out_ref, geo_ref = refs
    tile = lax.axis_index("tile")
    plane = lax.axis_index("plane")
    group = geo_ref.shape[0] // 4
    groups = cell_ref.shape[0] // group
    which = turn - plane
    active = (which >= 0) & (which < groups)
    span = float(tile_rows - 1)
    if turn:
        bend_ref[...] = bent(plane, inbox_a_ref[...], hess_ref[...])

    def came(g, axis, at, n):
        if not turn:
            return jnp.zeros((1, n), F32)
        return jnp.where(plane == 0, 0.0, inbox_ref[pl.ds(2 * g + axis, 1), pl.ds(at, n)])

    @pl.when(active)
    def _():
        rays = out_ref.shape[1]
        for g in range(group):
            batch = which * group + g
            cell = cell_ref[pl.ds(batch, 1), :]
            base_row = (tile * tile_rows + cell // NG).astype(F32) + offset_ref[0, pl.ds(batch, 1), :]
            base_col = (cell % NG).astype(F32) + offset_ref[1, pl.ds(batch, 1), :]
            row_pos = base_row + span * jnp.tanh(came(g, 0, 0, rays) / span)
            col_pos = base_col + span * jnp.tanh(came(g, 1, 0, rays) / span)
            row_floor = jnp.floor(row_pos)
            col_floor = jnp.floor(col_pos)
            geo_ref[4 * g : 4 * g + 1, :] = row_floor - ((tile - 1) * tile_rows).astype(F32)
            geo_ref[4 * g + 1 : 4 * g + 2, :] = row_pos - row_floor
            geo_ref[4 * g + 2 : 4 * g + 3, :] = col_floor
            geo_ref[4 * g + 3 : 4 * g + 4, :] = col_pos - col_floor

        def emit(g, at, n, values):
            for axis in (0, 1):
                out_ref[pl.ds(2 * g + axis, 1), pl.ds(at, n)] = (
                    came(g, axis, at, n) - LENS_WEIGHT * values[axis : axis + 1]
                )

        lookup(geo_ref, tab_ref, emit)

    @pl.when(jnp.logical_not(active))
    def _():
        out_ref[...] = jnp.zeros(out_ref.shape, F32)
        geo_ref[...] = jnp.zeros(geo_ref.shape, F32)


def hessian_kernel(geo_ref, tab_ref, out_ref, *, groups, turn):
    which = turn - lax.axis_index("plane")
    active = (which >= 0) & (which < groups)

    @pl.when(active)
    def _():
        def emit(g, at, n, values):
            for c in range(3):
                out_ref[pl.ds(3 * g + c, 1), pl.ds(at, n)] = values[c : c + 1]

        lookup(geo_ref, tab_ref, emit)

    @pl.when(jnp.logical_not(active))
    def _():
        out_ref[...] = jnp.zeros(out_ref.shape, F32)


def gather_kernel(*refs, planes, turns):
    pos_refs = refs[0:turns]
    bend_refs = refs[turns : 2 * turns - 1]
    inbox_a_ref, hess_ref, out_ref = refs[2 * turns - 1 :]
    plane = lax.axis_index("plane")
    group = hess_ref.shape[0] // 3
    groups = out_ref.shape[1] // group
    for p in range(planes):

        @pl.when(plane == p)
        def _():
            for j in range(groups):
                if p + j < len(bend_refs):
                    late = bend_refs[p + j][...]
                else:
                    late = bent(plane, inbox_a_ref[...], hess_ref[...])
                for i in range(group):
                    out_ref[0, j * group + i, 0:2, :] = pos_refs[p + j][2 * i : 2 * i + 2, :]
                    out_ref[0, j * group + i, 2:6, :] = late[4 * i : 4 * i + 4, :]


def per_device(block_dest, particle_cell, particle_offset, particle_mass, ray_cell, ray_offset):
    tiles = lax.axis_size("tile")
    planes = lax.axis_size("plane")
    tile_rows = NG // tiles
    tile_now = lax.axis_index("tile")
    plane_now = lax.axis_index("plane")
    blocks = particle_cell.shape[1]
    block_len = particle_cell.shape[2]
    cap = 2 * blocks // tiles
    win = 3 * tile_rows

    outgoing = pl.pallas_call(
        route_kernel,
        out_shape=jax.ShapeDtypeStruct((tiles * 4 * cap, block_len), F32),
        in_specs=[hbm_spec()] * 4,
        out_specs=vmem_spec(),
        scratch_shapes=[
            pltpu.SMEM((blocks,), jnp.int32),
            VMEM(particle_cell.shape, jnp.int32),
            VMEM(particle_offset.shape, F32),
            VMEM(particle_mass.shape, F32),
            pltpu.SMEM((tiles,), jnp.int32),
            pltpu.SemaphoreType.DMA((4,)),
        ],
        compiler_params=params(58),
        name="route",
    )(block_dest.reshape(-1), particle_cell, particle_offset, particle_mass)
    incoming = lax.all_to_all(
        outgoing.reshape(tiles, 4 * cap, block_len), "tile", split_axis=0, concat_axis=0, tiled=True
    )

    v_hi, v_lo, u_hi, u_lo = pl.pallas_call(
        tables_kernel,
        out_shape=(
            jax.ShapeDtypeStruct((NP, NG), BF16),
            jax.ShapeDtypeStruct((NP, NG), BF16),
            jax.ShapeDtypeStruct((2 * win, NP), BF16),
            jax.ShapeDtypeStruct((2 * win, NP), BF16),
        ),
        in_specs=[],
        out_specs=(vmem_spec(),) * 4,
        compiler_params=params(12),
        name="tables",
    )()

    scaling = math.sqrt(tile_rows * NG / (BLOCKS_DEV * block_len))
    rows_acc = -(-(tile_rows + 1) // 16) * 16
    canvas_rows = tile_rows + 8
    canvas = pl.pallas_call(
        lambda a, b, c: deposit_kernel(a, b, c, scaling=scaling, tile_rows=tile_rows),
        out_shape=jax.ShapeDtypeStruct((canvas_rows, NG), F32),
        in_specs=[vmem_spec()],
        out_specs=vmem_spec(),
        scratch_shapes=[VMEM((4 * rows_acc, NG), F32)],
        compiler_params=params(12),
        name="deposit",
    )(incoming)

    groups = [[i for i in range(tiles) if i % 2 == p] for p in (0, 1)]
    mine = lax.all_gather(canvas, "tile", axis=0, tiled=False, axis_index_groups=groups)
    other = lax.ppermute(mine, "tile", [(i, i ^ 1) for i in range(tiles)])

    shape = jax.ShapeDtypeStruct
    part, tab_a, ba, window, corner = pl.pallas_call(
        lambda *refs: fields_kernel(*refs, tile_rows=tile_rows),
        out_shape=(
            shape((2, tile_rows, NG), F32),
            shape((win // SUB, 2, SUB, 3 * NG), BF16),
            shape((2 * win, NP), F32),
            shape((win, NG), F32),
            shape((8, 128), F32),
        ),
        in_specs=[vmem_spec()] * 6,
        out_specs=(vmem_spec(),) * 5,
        scratch_shapes=[
            VMEM((NG + 2 * tile_rows, NG), F32),
            VMEM((NG, NG), BF16),
            VMEM((NG, NG), BF16),
            VMEM((2 * win, NP), BF16),
            VMEM((2 * win, NP), BF16),
        ],
        compiler_params=params(24),
        name="fields",
    )(mine, other, v_hi, v_lo, u_hi, u_lo)
    lens, tab_h = pl.pallas_call(
        lambda *refs: second_kernel(*refs, tile_rows=tile_rows),
        out_shape=(
            shape((1, 5, tile_rows, NG), F32),
            shape((win // SUB, 3, SUB, 3 * NG), BF16),
        ),
        in_specs=[vmem_spec()] * 6,
        out_specs=(vmem_spec(),) * 2,
        scratch_shapes=[VMEM((3 * win, NP), BF16), VMEM((3 * win, NP), BF16)],
        compiler_params=params(16),
        name="second",
    )(ba, window, corner, part, v_hi, v_lo)

    batches = ray_cell.shape[0]
    rays = ray_cell.shape[1]
    groups_b = batches // GROUP
    ring = [(i, (i + 1) % planes) for i in range(planes)]
    turns = groups_b + planes - 1
    received = ()
    positions = []
    bends = []
    inbox_a = jnp.zeros((4 * GROUP, rays), F32)
    for turn in range(turns):
        out_shape = [shape((2 * GROUP, rays), F32), shape((4 * GROUP, rays), F32)]
        if turn:
            out_shape.append(shape((4 * GROUP, rays), F32))
        moved = pl.pallas_call(
            lambda *refs, turn=turn: move_kernel(*refs, tile_rows=tile_rows, turn=turn),
            out_shape=tuple(out_shape),
            in_specs=[vmem_spec()] * (len(received) + 3),
            out_specs=(vmem_spec(),) * len(out_shape),
            compiler_params=params(16),
            name=f"move{turn}",
        )(*received, ray_cell, ray_offset, tab_a)
        positions.append(moved[0])
        inbox = None
        if turn < turns - 1:
            inbox = lax.ppermute(moved[0], "plane", ring)
        if turn:
            bends.append(moved[1])
            inbox_a = lax.ppermute(moved[1], "plane", ring)
        hess = pl.pallas_call(
            lambda *refs, turn=turn: hessian_kernel(*refs, groups=groups_b, turn=turn),
            out_shape=shape((3 * GROUP, rays), F32),
            in_specs=[vmem_spec()] * 2,
            out_specs=vmem_spec(),
            compiler_params=params(16),
            name=f"hessian{turn}",
        )(moved[-1], tab_h)
        received = (inbox, inbox_a, hess)
    ray_maps = pl.pallas_call(
        lambda *refs: gather_kernel(*refs, planes=planes, turns=turns),
        out_shape=shape((1, batches, 6, rays), F32),
        in_specs=[vmem_spec()] * (2 * turns + 1),
        out_specs=vmem_spec(),
        compiler_params=params(8),
        name="gather",
    )(*positions, *bends, inbox_a, received[2])
    return (lens, ray_maps)


def solution(mesh):
    return jax.shard_map(
        per_device,
        mesh=mesh,
        in_specs=(
            P("plane", "tile", None),
            P("plane", "tile", None),
            P("plane", None, "tile", None),
            P("plane", "tile", None),
            P(None, "tile"),
            P(None, None, "tile"),
        ),
        out_specs=(P("plane", None, "tile", None), P("plane", None, None, "tile")),
        check_vma=False,
    )
```

```python
import math

import jax
import jax.numpy as jnp
from jax import lax
from jax.experimental import pallas as pl
from jax.experimental.pallas import tpu as pltpu
from jax.sharding import PartitionSpec as P

NG = 512
NP = 2 * NG
HALF = NP // 2
BLOCKS_DEV = 64

LENS_WEIGHT = 0.15
SCREEN_SCALE = 0.5
MU2 = (SCREEN_SCALE * 2.0 * math.pi / NP) ** 2
WAVE = 2.0 * math.pi / NP
F32 = jnp.float32
BF16 = jnp.bfloat16
VMEM = pltpu.VMEM
RAY_CHUNK = 1024
GROUP = 2
SUB = 16
TIERS = (5, 6)
STEP = 4


def vmem_spec():
    return pl.BlockSpec(memory_space=pltpu.VMEM)


def hbm_spec():
    return pl.BlockSpec(memory_space=pltpu.HBM)


def params(mib):
    return pltpu.CompilerParams(vmem_limit_bytes=mib * 1024 * 1024)


def smem_spec():
    return pl.BlockSpec(memory_space=pltpu.SMEM)


def split(x):
    hi = x.astype(BF16)
    return hi, (x - hi.astype(F32)).astype(BF16)


def dot_nt(a, b):
    return lax.dot_general(a, b, (((1,), (1,)), ((), ())), preferred_element_type=F32)


def dot_nn(a, b):
    return lax.dot_general(a, b, (((1,), (0,)), ((), ())), preferred_element_type=F32)


def route_kernel(dest_hbm, cell_hbm, offset_hbm, mass_hbm, out_ref, dest_ref, cell_ref, offset_ref, mass_ref, count_ref, sems):
    copies = [
        pltpu.make_async_copy(src, dst, sems.at[i])
        for i, (src, dst) in enumerate(
            (
                (dest_hbm, dest_ref),
                (cell_hbm, cell_ref),
                (offset_hbm, offset_ref),
                (mass_hbm, mass_ref),
            )
        )
    ]
    for copy in copies:
        copy.start()
    tiles = count_ref.shape[0]
    blocks = cell_ref.shape[1]
    cap = out_ref.shape[0] // (4 * tiles)
    out_ref[...] = jnp.zeros(out_ref.shape, F32)
    for t in range(tiles):
        count_ref[t] = 0
    for copy in copies:
        copy.wait()

    def place(i, carry):
        dest = dest_ref[i]
        rank = count_ref[dest]
        count_ref[dest] = rank + 1
        row = dest * (4 * cap) + rank
        out_ref[pl.ds(row, 1), :] = cell_ref[0, pl.ds(i, 1), :].astype(F32)
        out_ref[pl.ds(row + cap, 1), :] = offset_ref[0, 0, pl.ds(i, 1), :]
        out_ref[pl.ds(row + 2 * cap, 1), :] = offset_ref[0, 1, pl.ds(i, 1), :]
        out_ref[pl.ds(row + 3 * cap, 1), :] = mass_ref[0, pl.ds(i, 1), :]
        return carry

    lax.fori_loop(0, blocks, place, 0)


def deposit_kernel(in_ref, out_ref, acc_ref, *, scaling, tile_rows):
    tiles = in_ref.shape[0]
    cap = in_ref.shape[1] // 4
    lanes = in_ref.shape[2]
    group = min(8, cap)
    rows = -(-(tile_rows + 1) // 16) * 16
    acc_ref[...] = jnp.zeros(acc_ref.shape, F32)
    row_iota = lax.broadcasted_iota(jnp.int32, (rows, lanes), 0).astype(F32).astype(BF16)
    col_iota = (lax.broadcasted_iota(jnp.int32, (NG, lanes), 0) - NG // 2).astype(F32).astype(BF16)
    zero = jnp.zeros((), BF16)
    one = jnp.ones((), BF16)

    def step(src, start):
        pieces_r = []
        pieces_c = []
        for j in range(start, start + group):
            cell = in_ref[src, pl.ds(j, 1), :].astype(jnp.int32)
            frac_r = in_ref[src, pl.ds(cap + j, 1), :]
            frac_c = in_ref[src, pl.ds(2 * cap + j, 1), :]
            mass = in_ref[src, pl.ds(3 * cap + j, 1), :]
            row_id = (cell // NG).astype(F32)
            col_id = (cell % NG - NG // 2).astype(F32).astype(BF16)
            first = row_iota == row_id.astype(BF16)
            second = row_iota == (row_id + 1.0).astype(BF16)
            upper = mass * (1.0 - frac_r)
            lower = mass * frac_r
            rows_now = []
            for side in (1.0 - frac_c, frac_c):
                a_hi, a_lo = split(upper * side)
                b_hi, b_lo = split(lower * side)
                rows_now.append(jnp.where(first, a_hi, jnp.where(second, b_hi, zero)))
                rows_now.append(jnp.where(first, a_lo, jnp.where(second, b_lo, zero)))
            pieces_r.append(jnp.concatenate(rows_now, axis=0))
            pieces_c.append(jnp.where(col_iota == col_id, one, zero))
        acc_ref[...] += dot_nt(jnp.concatenate(pieces_r, axis=1), jnp.concatenate(pieces_c, axis=1))

    def per_source(src, carry):
        step(src, 0)
        for start in range(group, cap, group):
            block = in_ref[src, pl.ds(3 * cap + start, group), :]

            @pl.when(jnp.max(jnp.abs(block)) > 0.0)
            def _():
                step(src, start)

        return carry

    lax.fori_loop(0, tiles, per_source, 0)
    near = acc_ref[0:rows, :] + acc_ref[rows : 2 * rows, :]
    far = acc_ref[2 * rows : 3 * rows, :] + acc_ref[3 * rows : 4 * rows, :]
    lane = lax.broadcasted_iota(jnp.int32, (rows, NG), 1)
    total = (near + jnp.where(lane == 0, 0.0, pltpu.roll(far, 1, 1))) * scaling
    out_ref[...] = total[0 : out_ref.shape[0], :]


def unit_circle(left, right):
    turn = (left * right % NP).astype(F32) * WAVE
    return jnp.cos(turn), jnp.sin(turn)


def tables_kernel(v_hi_ref, v_lo_ref, u_hi_ref, u_lo_ref):
    lanes = 128
    fine = 32
    shape = (HALF // fine, lanes)
    coarse_c, coarse_s = unit_circle(
        fine * lax.broadcasted_iota(jnp.int32, shape, 0), lax.broadcasted_iota(jnp.int32, shape, 1)
    )
    shape = (fine, lanes)
    fine_c, fine_s = unit_circle(
        lax.broadcasted_iota(jnp.int32, shape, 0), lax.broadcasted_iota(jnp.int32, shape, 1)
    )
    parity = (1 - 2 * (lax.broadcasted_iota(jnp.int32, shape, 1) % 2)).astype(F32)
    first = lax.broadcasted_iota(jnp.int32, shape, 0) == 0
    for a in range(HALF // fine):
        ca = coarse_c[a : a + 1, :]
        sa = coarse_s[a : a + 1, :]
        base_cos = fine_c * ca - fine_s * sa
        base_sin = fine_s * ca + fine_c * sa
        k_index = a * fine + lax.broadcasted_iota(jnp.int32, shape, 0)
        for j in range(NG // lanes):
            q_cos, q_sin = 1.0, 0.0
            if j:
                step = NP // math.gcd(NP, lanes * j)
                turn = (k_index * (lanes * j)) % NP
                q_cos = jnp.ones(shape, F32)
                q_sin = jnp.zeros(shape, F32)
                for q in range(1, step):
                    angle = 2.0 * math.pi * q / step
                    hit = turn == q * (NP // step)
                    q_cos = jnp.where(hit, math.cos(angle), q_cos)
                    q_sin = jnp.where(hit, math.sin(angle), q_sin)
            cos_now = base_cos * q_cos - base_sin * q_sin
            sin_now = base_sin * q_cos + base_cos * q_sin
            if a == 0:
                sin_now = jnp.where(first, parity, sin_now)
            for at, value in ((0, cos_now), (HALF, sin_now)):
                hi, lo = split(value)
                v_hi_ref[at + a * fine : at + (a + 1) * fine, j * lanes : (j + 1) * lanes] = hi
                v_lo_ref[at + a * fine : at + (a + 1) * fine, j * lanes : (j + 1) * lanes] = lo
    win = u_hi_ref.shape[0] // 2
    fine = 16
    shape = (fine, HALF)
    fine_c, fine_s = unit_circle(
        lax.broadcasted_iota(jnp.int32, shape, 0), lax.broadcasted_iota(jnp.int32, shape, 1)
    )
    lane = lax.broadcasted_iota(jnp.int32, shape, 1)
    wave = lane.astype(F32) * WAVE
    parity = (1 - 2 * (lax.broadcasted_iota(jnp.int32, shape, 0) % 2)).astype(F32)
    for a in range(win // fine):
        ca, sa = unit_circle(jnp.full((1, HALF), a * fine, jnp.int32), lane[0:1])
        w_cos = fine_c * ca - fine_s * sa
        w_sin = fine_s * ca + fine_c * sa
        for rows, cols, value in (
            (0, 0, w_cos),
            (0, HALF, jnp.where(lane == 0, parity, w_sin)),
            (win, 0, -wave * w_sin),
            (win, HALF, wave * w_cos),
        ):
            hi, lo = split(value)
            u_hi_ref[rows + a * fine : rows + (a + 1) * fine, cols : cols + HALF] = hi
            u_lo_ref[rows + a * fine : rows + (a + 1) * fine, cols : cols + HALF] = lo


def fields_kernel(
    canvas_refs,
    v_hi_ref,
    v_lo_ref,
    u_hi_ref,
    u_lo_ref,
    lens_ref,
    tab_ref,
    ba_ref,
    window_ref,
    corner_ref,
    dens_ref,
    dens_hi_ref,
    dens_lo_ref,
    l_hi_ref,
    l_lo_ref,
    *,
    tile_rows,
):
    tile = lax.axis_index("tile")
    tiles = len(canvas_refs)
    win = 3 * tile_rows
    pad = tile_rows
    zeros = jnp.zeros((pad, NG), F32)
    dens_ref[0:pad, :] = zeros
    dens_ref[pad + NG : pad + NG + pad, :] = zeros
    for e, src in enumerate(canvas_refs):
        row = pl.multiple_of(pad + jnp.bitwise_xor(tile, e) * tile_rows, 8)
        dens_ref[pl.ds(row, tile_rows), :] = src[0:tile_rows, :]
    for e, src in enumerate(canvas_refs):
        below = jnp.bitwise_xor(tile, e) + 1
        row = pl.multiple_of(pad + below * tile_rows, 8)
        dens_ref[pl.ds(row, 8), :] += jnp.where(below < tiles, src[tile_rows : tile_rows + 8, :], 0.0)
    d_hi, d_lo = split(dens_ref[pad : pad + NG, :])
    dens_hi_ref[...] = d_hi
    dens_lo_ref[...] = d_lo

    half_lane = lax.broadcasted_iota(jnp.int32, (1, HALF), 1).astype(F32) * WAVE
    origin = (tile - 1) * tile_rows + NP
    turn = (lax.broadcasted_iota(jnp.int32, (1, HALF), 1) * origin % NP).astype(F32) * WAVE
    turn_cos = jnp.cos(turn)
    turn_sin = jnp.sin(turn)
    lane = lax.broadcasted_iota(jnp.int32, (1, NP), 1)
    k_slot = jnp.where(lane < HALF, lane, jnp.where(lane == HALF, HALF, lane - HALF))
    kx = k_slot.astype(F32) * WAVE
    kx2 = kx * kx
    edge_k = (lane == 0) | (lane == HALF)
    weight_k = jnp.where(edge_k, 1.0, 2.0)
    block = 256

    def channel_block(i, corner):
        at = pl.multiple_of(i * block, block)
        v_hi = v_hi_ref[pl.ds(at, block), :]
        v_lo = v_lo_ref[pl.ds(at, block), :]
        dh = dens_hi_ref[...]
        first = dot_nt(v_hi, dh) + dot_nt(v_lo, dh) + dot_nt(v_hi, dens_lo_ref[...])
        f_hi, f_lo = split(first)
        spec = (
            dot_nt(f_hi, v_hi_ref[...]) + dot_nt(f_lo, v_hi_ref[...]) + dot_nt(f_hi, v_lo_ref[...])
        )
        chan = at + lax.broadcasted_iota(jnp.int32, (block, 1), 0)
        l_slot = jnp.where(chan < HALF, chan, jnp.where(chan == HALF, HALF, chan - HALF))
        ky = l_slot.astype(F32) * WAVE
        weight_l = jnp.where((chan == 0) | (chan == HALF), 1.0, 2.0)
        scale = (weight_l * (-2.0 / (NP * NP))) * weight_k
        pot = spec * (scale / (kx2 + ky * ky + MU2))
        corner = jnp.where(i == HALF // block, pot[0:1, HALF : HALF + 1], corner)
        pot_c = pot[:, 0:HALF]
        pot_s = pot[:, HALF:NP]
        turned = jnp.concatenate(
            [pot_c * turn_cos + pot_s * turn_sin, pot_s * turn_cos - pot_c * turn_sin], axis=1
        )
        p_hi, p_lo = split(turned)
        uh = u_hi_ref[...]
        ba_ref[:, pl.ds(at, block)] = (
            dot_nt(uh, p_hi) + dot_nt(u_lo_ref[...], p_hi) + dot_nt(uh, p_lo)
        )
        return corner

    corner = lax.fori_loop(0, NP // block, channel_block, jnp.zeros((1, 1), F32))

    row_at = lax.broadcasted_iota(jnp.int32, (win, 1), 0)
    grid_row = (tile - 1) * tile_rows + row_at
    inside = ((grid_row >= 0) & (grid_row < NG)).astype(F32)
    b_all = ba_ref[0:win, :] * inside
    a_all = ba_ref[win : 2 * win, :] * inside
    ba_ref[0:win, :] = b_all
    ba_ref[win : 2 * win, :] = a_all
    window_ref[...] = dens_ref[pl.ds(pl.multiple_of(tile * tile_rows, 8), win), :]
    corner_ref[...] = jnp.broadcast_to(corner * (-math.pi * math.pi), corner_ref.shape)
    slope = jnp.concatenate([half_lane * b_all[:, HALF:NP], -half_lane * b_all[:, 0:HALF]], axis=1)
    for f, value in enumerate((a_all, slope)):
        hi, lo = split(value)
        l_hi_ref[f * win : (f + 1) * win, :] = hi
        l_lo_ref[f * win : (f + 1) * win, :] = lo
    finish(2, l_hi_ref, l_lo_ref, v_hi_ref, v_lo_ref, None, lens_ref, tab_ref, tile_rows)


def finish(count, l_hi_ref, l_lo_ref, v_hi_ref, v_lo_ref, extra_ref, lens_ref, tab_ref, tile_rows):
    win = 3 * tile_rows
    shape = (win // SUB, SUB, NG)
    vh = v_hi_ref[...]
    out = dot_nn(l_hi_ref[...], vh) + dot_nn(l_lo_ref[...], vh) + dot_nn(l_hi_ref[...], v_lo_ref[...])
    at = lens_ref.shape[-3] - count
    for f in range(count):
        value = out[f * win : (f + 1) * win, :]
        if f == 0 and extra_ref is not None:
            value = value + 2.0 * extra_ref[...]
        lens_ref[..., at + f, :, :] = value[tile_rows : 2 * tile_rows, :].reshape(
            (1,) * (len(lens_ref.shape) - 3) + (tile_rows, NG)
        )
        hi, lo = split(value)
        tab_ref[:, f, :, 0:NG] = hi.reshape(shape)
        tab_ref[:, f, :, NG : 2 * NG] = lo.reshape(shape)
        tab_ref[:, f, :, 2 * NG : 3 * NG] = hi.reshape(shape)


def second_kernel(
    ba_ref,
    window_ref,
    corner_ref,
    part_ref,
    v_hi_ref,
    v_lo_ref,
    lens_ref,
    tab_ref,
    l_hi_ref,
    l_lo_ref,
    *,
    tile_rows,
):
    tile = lax.axis_index("tile")
    win = 3 * tile_rows
    lens_ref[0, 0:2] = part_ref[...]
    row_at = lax.broadcasted_iota(jnp.int32, (win, 1), 0)
    grid_row = (tile - 1) * tile_rows + row_at
    inside = ((grid_row >= 0) & (grid_row < NG)).astype(F32)
    corner_col = inside * (1 - 2 * (row_at % 2)).astype(F32) * corner_ref[0:1, 0:1]
    lane = lax.broadcasted_iota(jnp.int32, (1, NP), 1)
    slot = jnp.where(lane < HALF, lane, jnp.where(lane == HALF, HALF, lane - HALF))
    ky2 = (slot.astype(F32) * WAVE) * (slot.astype(F32) * WAVE)
    lane_half = lax.broadcasted_iota(jnp.int32, (1, HALF), 1)
    half_lane = lane_half.astype(F32) * WAVE
    b_all = ba_ref[0:win, :]
    a_cos = ba_ref[win : 2 * win, 0:HALF]
    a_sin = ba_ref[win : 2 * win, HALF:NP]
    mixed = jnp.concatenate(
        [half_lane * a_sin, jnp.where(lane_half == 0, corner_col, -half_lane * a_cos)], axis=1
    )
    for f, value in enumerate(((MU2 + ky2) * b_all, mixed, -ky2 * b_all)):
        hi, lo = split(value)
        l_hi_ref[f * win : (f + 1) * win, :] = hi
        l_lo_ref[f * win : (f + 1) * win, :] = lo
    finish(3, l_hi_ref, l_lo_ref, v_hi_ref, v_lo_ref, window_ref, lens_ref, tab_ref, tile_rows)


def lookup(geo_ref, tab_ref, emit, *, tile_rows, turn):
    chunks, fields, _, _ = tab_ref.shape
    group = geo_ref.shape[0] // 4
    rays = geo_ref.shape[1]
    n = min(RAY_CHUNK, rays)
    per = rays // n
    zero = jnp.zeros((), BF16)
    win = chunks * SUB
    least = float(win)
    most = 0.0
    for g in range(group):
        row_id = geo_ref[4 * g : 4 * g + 1, :]
        least = jnp.minimum(least, jnp.min(row_id))
        most = jnp.maximum(most, jnp.max(row_id))
    low = jnp.clip(least.astype(jnp.int32), 0, win - 1) // SUB
    high = jnp.clip(most.astype(jnp.int32) + 1, 0, win - 1) // SUB
    needed = high - low + 1
    tiers = sorted({min(t, chunks) for t in TIERS})

    def with_tier(tier, passes):
        col_iota = (lax.broadcasted_iota(jnp.int32, (NG, n), 0) - NG // 2).astype(F32).astype(BF16)
        row_iota = lax.broadcasted_iota(jnp.int32, (tier * SUB, n), 0).astype(F32)

        def chunk(i, carry):
            g = i // per
            at = pl.multiple_of((i % per) * n, n)
            row_id = geo_ref[pl.ds(4 * g, 1), pl.ds(at, n)]
            frac_row = geo_ref[pl.ds(4 * g + 1, 1), pl.ds(at, n)]
            col_floor = geo_ref[pl.ds(4 * g + 2, 1), pl.ds(at, n)]
            frac_col = geo_ref[pl.ds(4 * g + 3, 1), pl.ds(at, n)]
            far = 4.0 * NG
            c0 = jnp.where((col_floor >= 0.0) & (col_floor < NG), col_floor - NG // 2, far)
            c1 = jnp.where(
                (col_floor >= -1.0) & (col_floor < NG - 1.0), col_floor + (1.0 - NG // 2), far
            )
            here = col_iota == c0.astype(BF16)
            there = col_iota == c1.astype(BF16)
            g0_hi, g0_lo = split(1.0 - frac_col)
            g1_hi, g1_lo = split(frac_col)
            w_hi = jnp.where(here, g0_hi, jnp.where(there, g1_hi, zero))
            w_lo = jnp.where(here, g0_lo, jnp.where(there, g1_lo, zero))
            w = jnp.concatenate([w_hi, w_hi, w_lo], axis=0)

            def rows_from(start, floor):
                here_row = row_id - (start * SUB).astype(F32)
                row_w = jnp.where(row_iota == here_row, 1.0 - frac_row, 0.0) + jnp.where(
                    row_iota == here_row + 1.0, frac_row, 0.0
                )
                if floor is not None:
                    row_w = jnp.where(row_iota >= floor, row_w, 0.0)
                table = tab_ref[pl.ds(start, tier)].reshape(tier * fields * SUB, 3 * NG)
                along = dot_nn(table, w).reshape(tier, fields, SUB, n)
                values = jnp.sum(along * row_w.reshape(tier, 1, SUB, n), axis=0)
                return jnp.sum(values, axis=1)

            if passes is None:
                values = rows_from(jnp.minimum(low, chunks - tier), None)
            else:

                def one_pass(q, total):
                    begin = low + q * tier
                    start = jnp.minimum(begin, chunks - tier)
                    return total + rows_from(start, ((begin - start) * SUB).astype(F32))

                values = lax.fori_loop(0, passes, one_pass, jnp.zeros((fields, n), F32))
            emit(g, at, n, values)
            return carry

        lax.fori_loop(0, group * per, chunk, 0)

    still = (2 * tile_rows + 1) // SUB - tile_rows // SUB + 1
    if turn == 0:
        with_tier(still, None)
        return
    if turn > 1:
        tiers = [t for t in tiers if t > still] or tiers[-1:]
    floor = 0
    for tier in tiers:
        pl.when((needed > floor) & (needed <= tier))(lambda tier=tier: with_tier(tier, None))
        floor = tier
    if floor < chunks:
        pl.when(needed > floor)(lambda: with_tier(STEP, (needed + STEP - 1) // STEP))


def bent(plane, inbox_a, hess):
    rows = []
    for i in range(hess.shape[0] // 3):
        hxx = hess[3 * i : 3 * i + 1]
        hxy = hess[3 * i + 1 : 3 * i + 2]
        hyy = hess[3 * i + 2 : 3 * i + 3]
        first = plane == 0
        a11, a12, a21, a22 = (
            jnp.where(first, start, inbox_a[4 * i + c : 4 * i + c + 1])
            for c, start in enumerate((1.0, 0.0, 0.0, 1.0))
        )
        rows += [
            a11 - LENS_WEIGHT * (hxx * a11 + hxy * a21),
            a12 - LENS_WEIGHT * (hxx * a12 + hxy * a22),
            a21 - LENS_WEIGHT * (hxy * a11 + hyy * a21),
            a22 - LENS_WEIGHT * (hxy * a12 + hyy * a22),
        ]
    return jnp.concatenate(rows, axis=0)


def move_kernel(*refs, tile_rows, turn):
    if turn:
        inbox_ref, inbox_a_ref, hess_ref, cell_ref, offset_ref, tab_ref, out_ref, bend_ref, geo_ref = refs
    else:
        cell_ref, offset_ref, tab_ref, out_ref, geo_ref = refs
    tile = lax.axis_index("tile")
    plane = lax.axis_index("plane")
    group = geo_ref.shape[0] // 4
    groups = cell_ref.shape[0] // group
    which = turn - plane
    active = (which >= 0) & (which < groups)
    span = float(tile_rows - 1)
    if turn:
        bend_ref[...] = bent(plane, inbox_a_ref[...], hess_ref[...])

    def came(g, axis, at, n):
        if not turn:
            return jnp.zeros((1, n), F32)
        return jnp.where(plane == 0, 0.0, inbox_ref[pl.ds(2 * g + axis, 1), pl.ds(at, n)])

    @pl.when(active)
    def _():
        rays = out_ref.shape[1]
        for g in range(group):
            batch = which * group + g
            cell = cell_ref[pl.ds(batch, 1), :]
            base_row = (tile * tile_rows + cell // NG).astype(F32) + offset_ref[0, pl.ds(batch, 1), :]
            base_col = (cell % NG).astype(F32) + offset_ref[1, pl.ds(batch, 1), :]
            row_pos = base_row + span * jnp.tanh(came(g, 0, 0, rays) / span)
            col_pos = base_col + span * jnp.tanh(came(g, 1, 0, rays) / span)
            row_floor = jnp.floor(row_pos)
            col_floor = jnp.floor(col_pos)
            geo_ref[4 * g : 4 * g + 1, :] = row_floor - ((tile - 1) * tile_rows).astype(F32)
            geo_ref[4 * g + 1 : 4 * g + 2, :] = row_pos - row_floor
            geo_ref[4 * g + 2 : 4 * g + 3, :] = col_floor
            geo_ref[4 * g + 3 : 4 * g + 4, :] = col_pos - col_floor

        def emit(g, at, n, values):
            for axis in (0, 1):
                out_ref[pl.ds(2 * g + axis, 1), pl.ds(at, n)] = (
                    came(g, axis, at, n) - LENS_WEIGHT * values[axis : axis + 1]
                )

        lookup(geo_ref, tab_ref, emit, tile_rows=tile_rows, turn=turn)

    @pl.when(jnp.logical_not(active))
    def _():
        out_ref[...] = jnp.zeros(out_ref.shape, F32)
        geo_ref[...] = jnp.zeros(geo_ref.shape, F32)


def hessian_kernel(geo_ref, tab_ref, out_ref, *, groups, tile_rows, turn):
    which = turn - lax.axis_index("plane")
    active = (which >= 0) & (which < groups)

    @pl.when(active)
    def _():
        def emit(g, at, n, values):
            for c in range(3):
                out_ref[pl.ds(3 * g + c, 1), pl.ds(at, n)] = values[c : c + 1]

        lookup(geo_ref, tab_ref, emit, tile_rows=tile_rows, turn=turn)

    @pl.when(jnp.logical_not(active))
    def _():
        out_ref[...] = jnp.zeros(out_ref.shape, F32)


def gather_kernel(*refs, planes, turns):
    pos_refs = refs[0:turns]
    bend_refs = refs[turns : 2 * turns - 1]
    inbox_a_ref, hess_ref, out_ref = refs[2 * turns - 1 :]
    plane = lax.axis_index("plane")
    group = hess_ref.shape[0] // 3
    groups = out_ref.shape[1] // group
    for p in range(planes):

        @pl.when(plane == p)
        def _():
            for j in range(groups):
                if p + j < len(bend_refs):
                    late = bend_refs[p + j][...]
                else:
                    late = bent(plane, inbox_a_ref[...], hess_ref[...])
                for i in range(group):
                    out_ref[0, j * group + i, 0:2, :] = pos_refs[p + j][2 * i : 2 * i + 2, :]
                    out_ref[0, j * group + i, 2:6, :] = late[4 * i : 4 * i + 4, :]


def swapped(piece, e):
    tiles = lax.axis_size("tile")
    return lax.ppermute(piece, "tile", [(i, i ^ e) for i in range(tiles)])


def per_device(block_dest, particle_cell, particle_offset, particle_mass, ray_cell, ray_offset):
    tiles = lax.axis_size("tile")
    planes = lax.axis_size("plane")
    tile_rows = NG // tiles
    tile_now = lax.axis_index("tile")
    plane_now = lax.axis_index("plane")
    blocks = particle_cell.shape[1]
    block_len = particle_cell.shape[2]
    cap = 2 * blocks // tiles
    win = 3 * tile_rows

    outgoing = pl.pallas_call(
        route_kernel,
        out_shape=jax.ShapeDtypeStruct((tiles * 4 * cap, block_len), F32),
        in_specs=[hbm_spec()] * 4,
        out_specs=vmem_spec(),
        scratch_shapes=[
            pltpu.SMEM((blocks,), jnp.int32),
            VMEM(particle_cell.shape, jnp.int32),
            VMEM(particle_offset.shape, F32),
            VMEM(particle_mass.shape, F32),
            pltpu.SMEM((tiles,), jnp.int32),
            pltpu.SemaphoreType.DMA((4,)),
        ],
        compiler_params=params(58),
        name="route",
    )(block_dest.reshape(-1), particle_cell, particle_offset, particle_mass)
    incoming = lax.all_to_all(
        outgoing.reshape(tiles, 4 * cap, block_len), "tile", split_axis=0, concat_axis=0, tiled=True
    )

    v_hi, v_lo, u_hi, u_lo = pl.pallas_call(
        tables_kernel,
        out_shape=(
            jax.ShapeDtypeStruct((NP, NG), BF16),
            jax.ShapeDtypeStruct((NP, NG), BF16),
            jax.ShapeDtypeStruct((2 * win, NP), BF16),
            jax.ShapeDtypeStruct((2 * win, NP), BF16),
        ),
        in_specs=[],
        out_specs=(vmem_spec(),) * 4,
        compiler_params=params(12),
        name="tables",
    )()

    scaling = math.sqrt(tile_rows * NG / (BLOCKS_DEV * block_len))
    rows_acc = -(-(tile_rows + 1) // 16) * 16
    canvas_rows = tile_rows + 8
    canvas = pl.pallas_call(
        lambda a, b, c: deposit_kernel(a, b, c, scaling=scaling, tile_rows=tile_rows),
        out_shape=jax.ShapeDtypeStruct((canvas_rows, NG), F32),
        in_specs=[vmem_spec()],
        out_specs=vmem_spec(),
        scratch_shapes=[VMEM((4 * rows_acc, NG), F32)],
        compiler_params=params(12),
        name="deposit",
    )(incoming)

    near = [swapped(canvas, e) for e in range(2, tiles, 2)]
    v_hi, v_lo, u_hi, u_lo, *near = lax.optimization_barrier((v_hi, v_lo, u_hi, u_lo, *near))
    near = [canvas] + near
    canvases = [None] * tiles
    for d, piece in enumerate(near):
        canvases[2 * d] = piece
        canvases[2 * d + 1] = swapped(piece, 1)

    shape = jax.ShapeDtypeStruct
    part, tab_a, ba, window, corner = pl.pallas_call(
        lambda *refs: fields_kernel(refs[:tiles], *refs[tiles:], tile_rows=tile_rows),
        out_shape=(
            shape((2, tile_rows, NG), F32),
            shape((win // SUB, 2, SUB, 3 * NG), BF16),
            shape((2 * win, NP), F32),
            shape((win, NG), F32),
            shape((8, 128), F32),
        ),
        in_specs=[vmem_spec()] * (tiles + 4),
        out_specs=(vmem_spec(),) * 5,
        scratch_shapes=[
            VMEM((NG + 2 * tile_rows, NG), F32),
            VMEM((NG, NG), BF16),
            VMEM((NG, NG), BF16),
            VMEM((2 * win, NP), BF16),
            VMEM((2 * win, NP), BF16),
        ],
        compiler_params=params(24),
        name="fields",
    )(*canvases, v_hi, v_lo, u_hi, u_lo)
    lens, tab_h = pl.pallas_call(
        lambda *refs: second_kernel(*refs, tile_rows=tile_rows),
        out_shape=(
            shape((1, 5, tile_rows, NG), F32),
            shape((win // SUB, 3, SUB, 3 * NG), BF16),
        ),
        in_specs=[vmem_spec()] * 6,
        out_specs=(vmem_spec(),) * 2,
        scratch_shapes=[VMEM((3 * win, NP), BF16), VMEM((3 * win, NP), BF16)],
        compiler_params=params(16),
        name="second",
    )(ba, window, corner, part, v_hi, v_lo)

    batches = ray_cell.shape[0]
    rays = ray_cell.shape[1]
    groups_b = batches // GROUP
    ring = [(i, (i + 1) % planes) for i in range(planes)]
    turns = groups_b + planes - 1
    received = ()
    positions = []
    bends = []
    inbox_a = jnp.zeros((4 * GROUP, rays), F32)
    for turn in range(turns):
        out_shape = [shape((2 * GROUP, rays), F32), shape((4 * GROUP, rays), F32)]
        if turn:
            out_shape.append(shape((4 * GROUP, rays), F32))
        moved = pl.pallas_call(
            lambda *refs, turn=turn: move_kernel(*refs, tile_rows=tile_rows, turn=turn),
            out_shape=tuple(out_shape),
            in_specs=[vmem_spec()] * (len(received) + 3),
            out_specs=(vmem_spec(),) * len(out_shape),
            compiler_params=params(16),
            name=f"move{turn}",
        )(*received, ray_cell, ray_offset, tab_a)
        positions.append(moved[0])
        inbox = None
        if turn < turns - 1:
            inbox = lax.ppermute(moved[0], "plane", ring)
        if turn:
            bends.append(moved[1])
            inbox_a = lax.ppermute(moved[1], "plane", ring)
        hess = pl.pallas_call(
            lambda *refs, turn=turn: hessian_kernel(
                *refs, groups=groups_b, tile_rows=tile_rows, turn=turn
            ),
            out_shape=shape((3 * GROUP, rays), F32),
            in_specs=[vmem_spec()] * 2,
            out_specs=vmem_spec(),
            compiler_params=params(16),
            name=f"hessian{turn}",
        )(moved[-1], tab_h)
        received = (inbox, inbox_a, hess)
    ray_maps = pl.pallas_call(
        lambda *refs: gather_kernel(*refs, planes=planes, turns=turns),
        out_shape=shape((1, batches, 6, rays), F32),
        in_specs=[vmem_spec()] * (2 * turns + 1),
        out_specs=vmem_spec(),
        compiler_params=params(8),
        name="gather",
    )(*positions, *bends, inbox_a, received[2])
    return (lens, ray_maps)


def solution(mesh):
    return jax.shard_map(
        per_device,
        mesh=mesh,
        in_specs=(
            P("plane", "tile", None),
            P("plane", "tile", None),
            P("plane", None, "tile", None),
            P("plane", "tile", None),
            P(None, "tile"),
            P(None, None, "tile"),
        ),
        out_specs=(P("plane", None, "tile", None), P("plane", None, None, "tile")),
        check_vma=False,
    )
```

```python
import math

import jax
import jax.numpy as jnp
from jax import lax
from jax.experimental import pallas as pl
from jax.experimental.pallas import tpu as pltpu
from jax.sharding import PartitionSpec as P

NG = 512
NP = 2 * NG
HALF = NP // 2
BLOCKS_DEV = 64

LENS_WEIGHT = 0.15
SCREEN_SCALE = 0.5
MU2 = (SCREEN_SCALE * 2.0 * math.pi / NP) ** 2
WAVE = 2.0 * math.pi / NP
F32 = jnp.float32
BF16 = jnp.bfloat16
VMEM = pltpu.VMEM
RAY_CHUNK = 1024
GROUP = 2
SUB = 16
TIERS = (5, 6)
STEP = 4


def vmem_spec():
    return pl.BlockSpec(memory_space=pltpu.VMEM)


def hbm_spec():
    return pl.BlockSpec(memory_space=pltpu.HBM)


def params(mib):
    return pltpu.CompilerParams(vmem_limit_bytes=mib * 1024 * 1024)


def smem_spec():
    return pl.BlockSpec(memory_space=pltpu.SMEM)


def split(x):
    hi = x.astype(BF16)
    return hi, (x - hi.astype(F32)).astype(BF16)


def dot_nt(a, b):
    return lax.dot_general(a, b, (((1,), (1,)), ((), ())), preferred_element_type=F32)


def dot_nn(a, b):
    return lax.dot_general(a, b, (((1,), (0,)), ((), ())), preferred_element_type=F32)


def route_kernel(dest_hbm, cell_hbm, offset_hbm, mass_hbm, out_ref, dest_ref, cell_ref, offset_ref, mass_ref, count_ref, sems):
    copies = [
        pltpu.make_async_copy(src, dst, sems.at[i])
        for i, (src, dst) in enumerate(
            (
                (dest_hbm, dest_ref),
                (cell_hbm, cell_ref),
                (offset_hbm, offset_ref),
                (mass_hbm, mass_ref),
            )
        )
    ]
    for copy in copies:
        copy.start()
    tiles = count_ref.shape[0]
    blocks = cell_ref.shape[1]
    cap = out_ref.shape[0] // (4 * tiles)
    out_ref[...] = jnp.zeros(out_ref.shape, F32)
    for t in range(tiles):
        count_ref[t] = 0
    for copy in copies:
        copy.wait()

    def place(i, carry):
        dest = dest_ref[i]
        rank = count_ref[dest]
        count_ref[dest] = rank + 1
        row = dest * (4 * cap) + rank
        out_ref[pl.ds(row, 1), :] = cell_ref[0, pl.ds(i, 1), :].astype(F32)
        out_ref[pl.ds(row + cap, 1), :] = offset_ref[0, 0, pl.ds(i, 1), :]
        out_ref[pl.ds(row + 2 * cap, 1), :] = offset_ref[0, 1, pl.ds(i, 1), :]
        out_ref[pl.ds(row + 3 * cap, 1), :] = mass_ref[0, pl.ds(i, 1), :]
        return carry

    lax.fori_loop(0, blocks, place, 0)


def deposit_kernel(in_ref, out_ref, acc_ref, *, scaling, tile_rows):
    tiles = in_ref.shape[0]
    cap = in_ref.shape[1] // 4
    lanes = in_ref.shape[2]
    group = min(8, cap)
    rows = -(-(tile_rows + 1) // 16) * 16
    acc_ref[...] = jnp.zeros(acc_ref.shape, F32)
    row_iota = lax.broadcasted_iota(jnp.int32, (rows, lanes), 0).astype(F32).astype(BF16)
    col_iota = (lax.broadcasted_iota(jnp.int32, (NG, lanes), 0) - NG // 2).astype(F32).astype(BF16)
    zero = jnp.zeros((), BF16)
    one = jnp.ones((), BF16)

    def step(src, start):
        pieces_r = []
        pieces_c = []
        for j in range(start, start + group):
            cell = in_ref[src, pl.ds(j, 1), :].astype(jnp.int32)
            frac_r = in_ref[src, pl.ds(cap + j, 1), :]
            frac_c = in_ref[src, pl.ds(2 * cap + j, 1), :]
            mass = in_ref[src, pl.ds(3 * cap + j, 1), :]
            row_id = (cell // NG).astype(F32)
            col_id = (cell % NG - NG // 2).astype(F32).astype(BF16)
            first = row_iota == row_id.astype(BF16)
            second = row_iota == (row_id + 1.0).astype(BF16)
            upper = mass * (1.0 - frac_r)
            lower = mass * frac_r
            rows_now = []
            for side in (1.0 - frac_c, frac_c):
                a_hi, a_lo = split(upper * side)
                b_hi, b_lo = split(lower * side)
                rows_now.append(jnp.where(first, a_hi, jnp.where(second, b_hi, zero)))
                rows_now.append(jnp.where(first, a_lo, jnp.where(second, b_lo, zero)))
            pieces_r.append(jnp.concatenate(rows_now, axis=0))
            pieces_c.append(jnp.where(col_iota == col_id, one, zero))
        acc_ref[...] += dot_nt(jnp.concatenate(pieces_r, axis=1), jnp.concatenate(pieces_c, axis=1))

    def per_source(src, carry):
        step(src, 0)
        for start in range(group, cap, group):
            block = in_ref[src, pl.ds(3 * cap + start, group), :]

            @pl.when(jnp.max(jnp.abs(block)) > 0.0)
            def _():
                step(src, start)

        return carry

    lax.fori_loop(0, tiles, per_source, 0)
    near = acc_ref[0:rows, :] + acc_ref[rows : 2 * rows, :]
    far = acc_ref[2 * rows : 3 * rows, :] + acc_ref[3 * rows : 4 * rows, :]
    lane = lax.broadcasted_iota(jnp.int32, (rows, NG), 1)
    total = (near + jnp.where(lane == 0, 0.0, pltpu.roll(far, 1, 1))) * scaling
    out_ref[...] = total[0 : out_ref.shape[0], :]


def unit_circle(left, right):
    turn = (left * right % NP).astype(F32) * WAVE
    return jnp.cos(turn), jnp.sin(turn)


def tables_kernel(v_hi_ref, v_lo_ref, u_hi_ref, u_lo_ref):
    lanes = 128
    fine = 32
    shape = (HALF // fine, lanes)
    coarse_c, coarse_s = unit_circle(
        fine * lax.broadcasted_iota(jnp.int32, shape, 0), lax.broadcasted_iota(jnp.int32, shape, 1)
    )
    shape = (fine, lanes)
    fine_c, fine_s = unit_circle(
        lax.broadcasted_iota(jnp.int32, shape, 0), lax.broadcasted_iota(jnp.int32, shape, 1)
    )
    parity = (1 - 2 * (lax.broadcasted_iota(jnp.int32, shape, 1) % 2)).astype(F32)
    first = lax.broadcasted_iota(jnp.int32, shape, 0) == 0
    for a in range(HALF // fine):
        ca = coarse_c[a : a + 1, :]
        sa = coarse_s[a : a + 1, :]
        base_cos = fine_c * ca - fine_s * sa
        base_sin = fine_s * ca + fine_c * sa
        k_index = a * fine + lax.broadcasted_iota(jnp.int32, shape, 0)
        for j in range(NG // lanes):
            q_cos, q_sin = 1.0, 0.0
            if j:
                step = NP // math.gcd(NP, lanes * j)
                turn = (k_index * (lanes * j)) % NP
                q_cos = jnp.ones(shape, F32)
                q_sin = jnp.zeros(shape, F32)
                for q in range(1, step):
                    angle = 2.0 * math.pi * q / step
                    hit = turn == q * (NP // step)
                    q_cos = jnp.where(hit, math.cos(angle), q_cos)
                    q_sin = jnp.where(hit, math.sin(angle), q_sin)
            cos_now = base_cos * q_cos - base_sin * q_sin
            sin_now = base_sin * q_cos + base_cos * q_sin
            if a == 0:
                sin_now = jnp.where(first, parity, sin_now)
            for at, value in ((0, cos_now), (HALF, sin_now)):
                hi, lo = split(value)
                v_hi_ref[at + a * fine : at + (a + 1) * fine, j * lanes : (j + 1) * lanes] = hi
                v_lo_ref[at + a * fine : at + (a + 1) * fine, j * lanes : (j + 1) * lanes] = lo
    win = u_hi_ref.shape[0] // 2
    fine = 16
    shape = (fine, HALF)
    fine_c, fine_s = unit_circle(
        lax.broadcasted_iota(jnp.int32, shape, 0), lax.broadcasted_iota(jnp.int32, shape, 1)
    )
    lane = lax.broadcasted_iota(jnp.int32, shape, 1)
    wave = lane.astype(F32) * WAVE
    parity = (1 - 2 * (lax.broadcasted_iota(jnp.int32, shape, 0) % 2)).astype(F32)
    for a in range(win // fine):
        ca, sa = unit_circle(jnp.full((1, HALF), a * fine, jnp.int32), lane[0:1])
        w_cos = fine_c * ca - fine_s * sa
        w_sin = fine_s * ca + fine_c * sa
        for rows, cols, value in (
            (0, 0, w_cos),
            (0, HALF, jnp.where(lane == 0, parity, w_sin)),
            (win, 0, -wave * w_sin),
            (win, HALF, wave * w_cos),
        ):
            hi, lo = split(value)
            u_hi_ref[rows + a * fine : rows + (a + 1) * fine, cols : cols + HALF] = hi
            u_lo_ref[rows + a * fine : rows + (a + 1) * fine, cols : cols + HALF] = lo


def fields_kernel(
    canvas_refs,
    v_hi_ref,
    v_lo_ref,
    u_hi_ref,
    u_lo_ref,
    lens_ref,
    tab_ref,
    ba_ref,
    window_ref,
    corner_ref,
    dens_ref,
    dens_hi_ref,
    dens_lo_ref,
    l_hi_ref,
    l_lo_ref,
    *,
    tile_rows,
):
    tile = lax.axis_index("tile")
    tiles = len(canvas_refs)
    win = 3 * tile_rows
    pad = tile_rows
    zeros = jnp.zeros((pad, NG), F32)
    dens_ref[0:pad, :] = zeros
    dens_ref[pad + NG : pad + NG + pad, :] = zeros
    for e, src in enumerate(canvas_refs):
        row = pl.multiple_of(pad + jnp.bitwise_xor(tile, e) * tile_rows, 8)
        dens_ref[pl.ds(row, tile_rows), :] = src[0:tile_rows, :]
    for e, src in enumerate(canvas_refs):
        below = jnp.bitwise_xor(tile, e) + 1
        row = pl.multiple_of(pad + below * tile_rows, 8)
        dens_ref[pl.ds(row, 8), :] += jnp.where(below < tiles, src[tile_rows : tile_rows + 8, :], 0.0)
    d_hi, d_lo = split(dens_ref[pad : pad + NG, :])
    dens_hi_ref[...] = d_hi
    dens_lo_ref[...] = d_lo

    half_lane = lax.broadcasted_iota(jnp.int32, (1, HALF), 1).astype(F32) * WAVE
    origin = (tile - 1) * tile_rows + NP
    turn = (lax.broadcasted_iota(jnp.int32, (1, HALF), 1) * origin % NP).astype(F32) * WAVE
    turn_cos = jnp.cos(turn)
    turn_sin = jnp.sin(turn)
    lane = lax.broadcasted_iota(jnp.int32, (1, NP), 1)
    k_slot = jnp.where(lane < HALF, lane, jnp.where(lane == HALF, HALF, lane - HALF))
    kx = k_slot.astype(F32) * WAVE
    kx2 = kx * kx
    edge_k = (lane == 0) | (lane == HALF)
    weight_k = jnp.where(edge_k, 1.0, 2.0)
    block = 512

    def channel_block(i, corner):
        at = pl.multiple_of(i * block, block)
        v_hi = v_hi_ref[pl.ds(at, block), :]
        v_lo = v_lo_ref[pl.ds(at, block), :]
        dh = dens_hi_ref[...]
        first = dot_nt(v_hi, dh) + dot_nt(v_lo, dh) + dot_nt(v_hi, dens_lo_ref[...])
        f_hi, f_lo = split(first)
        spec = (
            dot_nt(f_hi, v_hi_ref[...]) + dot_nt(f_lo, v_hi_ref[...]) + dot_nt(f_hi, v_lo_ref[...])
        )
        chan = at + lax.broadcasted_iota(jnp.int32, (block, 1), 0)
        l_slot = jnp.where(chan < HALF, chan, jnp.where(chan == HALF, HALF, chan - HALF))
        ky = l_slot.astype(F32) * WAVE
        weight_l = jnp.where((chan == 0) | (chan == HALF), 1.0, 2.0)
        scale = (weight_l * (-2.0 / (NP * NP))) * weight_k
        pot = spec * (scale / (kx2 + ky * ky + MU2))
        corner = jnp.where(i == HALF // block, pot[0:1, HALF : HALF + 1], corner)
        pot_c = pot[:, 0:HALF]
        pot_s = pot[:, HALF:NP]
        turned = jnp.concatenate(
            [pot_c * turn_cos + pot_s * turn_sin, pot_s * turn_cos - pot_c * turn_sin], axis=1
        )
        p_hi, p_lo = split(turned)
        uh = u_hi_ref[...]
        ba_ref[:, pl.ds(at, block)] = (
            dot_nt(uh, p_hi) + dot_nt(u_lo_ref[...], p_hi) + dot_nt(uh, p_lo)
        )
        return corner

    corner = lax.fori_loop(0, NP // block, channel_block, jnp.zeros((1, 1), F32))

    row_at = lax.broadcasted_iota(jnp.int32, (win, 1), 0)
    grid_row = (tile - 1) * tile_rows + row_at
    inside = ((grid_row >= 0) & (grid_row < NG)).astype(F32)
    b_all = ba_ref[0:win, :] * inside
    a_all = ba_ref[win : 2 * win, :] * inside
    ba_ref[0:win, :] = b_all
    ba_ref[win : 2 * win, :] = a_all
    window_ref[...] = dens_ref[pl.ds(pl.multiple_of(tile * tile_rows, 8), win), :]
    corner_ref[...] = jnp.broadcast_to(corner * (-math.pi * math.pi), corner_ref.shape)
    slope = jnp.concatenate([half_lane * b_all[:, HALF:NP], -half_lane * b_all[:, 0:HALF]], axis=1)
    for f, value in enumerate((a_all, slope)):
        hi, lo = split(value)
        l_hi_ref[f * win : (f + 1) * win, :] = hi
        l_lo_ref[f * win : (f + 1) * win, :] = lo
    finish(2, l_hi_ref, l_lo_ref, v_hi_ref, v_lo_ref, None, lens_ref, tab_ref, tile_rows)


def finish(count, l_hi_ref, l_lo_ref, v_hi_ref, v_lo_ref, extra_ref, lens_ref, tab_ref, tile_rows):
    win = 3 * tile_rows
    shape = (win // SUB, SUB, NG)
    vh = v_hi_ref[...]
    out = dot_nn(l_hi_ref[...], vh) + dot_nn(l_lo_ref[...], vh) + dot_nn(l_hi_ref[...], v_lo_ref[...])
    at = lens_ref.shape[-3] - count
    for f in range(count):
        value = out[f * win : (f + 1) * win, :]
        if f == 0 and extra_ref is not None:
            value = value + 2.0 * extra_ref[...]
        lens_ref[..., at + f, :, :] = value[tile_rows : 2 * tile_rows, :].reshape(
            (1,) * (len(lens_ref.shape) - 3) + (tile_rows, NG)
        )
        hi, lo = split(value)
        tab_ref[:, f, :, 0:NG] = hi.reshape(shape)
        tab_ref[:, f, :, NG : 2 * NG] = lo.reshape(shape)
        tab_ref[:, f, :, 2 * NG : 3 * NG] = hi.reshape(shape)


def second_kernel(
    ba_ref,
    window_ref,
    corner_ref,
    part_ref,
    v_hi_ref,
    v_lo_ref,
    lens_ref,
    tab_ref,
    l_hi_ref,
    l_lo_ref,
    *,
    tile_rows,
):
    tile = lax.axis_index("tile")
    win = 3 * tile_rows
    lens_ref[0, 0:2] = part_ref[...]
    row_at = lax.broadcasted_iota(jnp.int32, (win, 1), 0)
    grid_row = (tile - 1) * tile_rows + row_at
    inside = ((grid_row >= 0) & (grid_row < NG)).astype(F32)
    corner_col = inside * (1 - 2 * (row_at % 2)).astype(F32) * corner_ref[0:1, 0:1]
    lane = lax.broadcasted_iota(jnp.int32, (1, NP), 1)
    slot = jnp.where(lane < HALF, lane, jnp.where(lane == HALF, HALF, lane - HALF))
    ky2 = (slot.astype(F32) * WAVE) * (slot.astype(F32) * WAVE)
    lane_half = lax.broadcasted_iota(jnp.int32, (1, HALF), 1)
    half_lane = lane_half.astype(F32) * WAVE
    b_all = ba_ref[0:win, :]
    a_cos = ba_ref[win : 2 * win, 0:HALF]
    a_sin = ba_ref[win : 2 * win, HALF:NP]
    mixed = jnp.concatenate(
        [half_lane * a_sin, jnp.where(lane_half == 0, corner_col, -half_lane * a_cos)], axis=1
    )
    for f, value in enumerate(((MU2 + ky2) * b_all, mixed, -ky2 * b_all)):
        hi, lo = split(value)
        l_hi_ref[f * win : (f + 1) * win, :] = hi
        l_lo_ref[f * win : (f + 1) * win, :] = lo
    finish(3, l_hi_ref, l_lo_ref, v_hi_ref, v_lo_ref, window_ref, lens_ref, tab_ref, tile_rows)


def lookup(geo_ref, tab_ref, emit, *, tile_rows, turn):
    chunks, fields, _, _ = tab_ref.shape
    group = geo_ref.shape[0] // 4
    rays = geo_ref.shape[1]
    n = min(RAY_CHUNK, rays)
    per = rays // n
    zero = jnp.zeros((), BF16)
    win = chunks * SUB
    least = float(win)
    most = 0.0
    for g in range(group):
        row_id = geo_ref[4 * g : 4 * g + 1, :]
        least = jnp.minimum(least, jnp.min(row_id))
        most = jnp.maximum(most, jnp.max(row_id))
    low = jnp.clip(least.astype(jnp.int32), 0, win - 1) // SUB
    high = jnp.clip(most.astype(jnp.int32) + 1, 0, win - 1) // SUB
    needed = high - low + 1
    tiers = sorted({min(t, chunks) for t in TIERS})

    def with_tier(tier, passes):
        col_iota = (lax.broadcasted_iota(jnp.int32, (NG, n), 0) - NG // 2).astype(F32).astype(BF16)
        row_iota = lax.broadcasted_iota(jnp.int32, (tier * SUB, n), 0).astype(F32)

        def chunk(i, carry):
            g = i // per
            at = pl.multiple_of((i % per) * n, n)
            row_id = geo_ref[pl.ds(4 * g, 1), pl.ds(at, n)]
            frac_row = geo_ref[pl.ds(4 * g + 1, 1), pl.ds(at, n)]
            col_floor = geo_ref[pl.ds(4 * g + 2, 1), pl.ds(at, n)]
            frac_col = geo_ref[pl.ds(4 * g + 3, 1), pl.ds(at, n)]
            far = 4.0 * NG
            c0 = jnp.where((col_floor >= 0.0) & (col_floor < NG), col_floor - NG // 2, far)
            c1 = jnp.where(
                (col_floor >= -1.0) & (col_floor < NG - 1.0), col_floor + (1.0 - NG // 2), far
            )
            here = col_iota == c0.astype(BF16)
            there = col_iota == c1.astype(BF16)
            g0_hi, g0_lo = split(1.0 - frac_col)
            g1_hi, g1_lo = split(frac_col)
            w_hi = jnp.where(here, g0_hi, jnp.where(there, g1_hi, zero))
            w_lo = jnp.where(here, g0_lo, jnp.where(there, g1_lo, zero))
            w = jnp.concatenate([w_hi, w_hi, w_lo], axis=0)

            def rows_from(start, floor):
                here_row = row_id - (start * SUB).astype(F32)
                row_w = jnp.where(row_iota == here_row, 1.0 - frac_row, 0.0) + jnp.where(
                    row_iota == here_row + 1.0, frac_row, 0.0
                )
                if floor is not None:
                    row_w = jnp.where(row_iota >= floor, row_w, 0.0)
                table = tab_ref[pl.ds(start, tier)].reshape(tier * fields * SUB, 3 * NG)
                along = dot_nn(table, w).reshape(tier, fields, SUB, n)
                values = jnp.sum(along * row_w.reshape(tier, 1, SUB, n), axis=0)
                return jnp.sum(values, axis=1)

            if passes is None:
                values = rows_from(jnp.minimum(low, chunks - tier), None)
            else:

                def one_pass(q, total):
                    begin = low + q * tier
                    start = jnp.minimum(begin, chunks - tier)
                    return total + rows_from(start, ((begin - start) * SUB).astype(F32))

                values = lax.fori_loop(0, passes, one_pass, jnp.zeros((fields, n), F32))
            emit(g, at, n, values)
            return carry

        lax.fori_loop(0, group * per, chunk, 0)

    still = (2 * tile_rows + 1) // SUB - tile_rows // SUB + 1
    if turn == 0:
        with_tier(still, None)
        return
    if turn > 1:
        tiers = [t for t in tiers if t > still] or tiers[-1:]
    floor = 0
    for tier in tiers:
        pl.when((needed > floor) & (needed <= tier))(lambda tier=tier: with_tier(tier, None))
        floor = tier
    if floor < chunks:
        pl.when(needed > floor)(lambda: with_tier(STEP, (needed + STEP - 1) // STEP))


def move_kernel(*refs, tile_rows, turn):
    if turn:
        inbox_ref, cell_ref, offset_ref, tab_ref, out_ref, geo_ref = refs
    else:
        cell_ref, offset_ref, tab_ref, out_ref, geo_ref = refs
    tile = lax.axis_index("tile")
    plane = lax.axis_index("plane")
    group = geo_ref.shape[0] // 4
    groups = cell_ref.shape[0] // group
    which = turn - plane
    active = (which >= 0) & (which < groups)
    span = float(tile_rows - 1)

    def came(g, axis, at, n):
        if not turn:
            return jnp.zeros((1, n), F32)
        return jnp.where(plane == 0, 0.0, inbox_ref[pl.ds(2 * g + axis, 1), pl.ds(at, n)])

    @pl.when(active)
    def _():
        rays = out_ref.shape[1]
        for g in range(group):
            batch = which * group + g
            cell = cell_ref[pl.ds(batch, 1), :]
            base_row = (tile * tile_rows + cell // NG).astype(F32) + offset_ref[0, pl.ds(batch, 1), :]
            base_col = (cell % NG).astype(F32) + offset_ref[1, pl.ds(batch, 1), :]
            row_pos = base_row + span * jnp.tanh(came(g, 0, 0, rays) / span)
            col_pos = base_col + span * jnp.tanh(came(g, 1, 0, rays) / span)
            row_floor = jnp.floor(row_pos)
            col_floor = jnp.floor(col_pos)
            geo_ref[4 * g : 4 * g + 1, :] = row_floor - ((tile - 1) * tile_rows).astype(F32)
            geo_ref[4 * g + 1 : 4 * g + 2, :] = row_pos - row_floor
            geo_ref[4 * g + 2 : 4 * g + 3, :] = col_floor
            geo_ref[4 * g + 3 : 4 * g + 4, :] = col_pos - col_floor

        def emit(g, at, n, values):
            for axis in (0, 1):
                out_ref[pl.ds(2 * g + axis, 1), pl.ds(at, n)] = (
                    came(g, axis, at, n) - LENS_WEIGHT * values[axis : axis + 1]
                )

        lookup(geo_ref, tab_ref, emit, tile_rows=tile_rows, turn=turn)

    @pl.when(jnp.logical_not(active))
    def _():
        out_ref[...] = jnp.zeros(out_ref.shape, F32)
        geo_ref[...] = jnp.zeros(geo_ref.shape, F32)


def bend_kernel(*refs, groups, tile_rows, turn):
    if turn:
        geo_ref, tab_ref, inbox_ref, out_ref = refs
    else:
        geo_ref, tab_ref, out_ref = refs
    plane = lax.axis_index("plane")
    which = turn - plane
    active = (which >= 0) & (which < groups)

    @pl.when(active)
    def _():
        def emit(g, at, n, values):
            hxx = values[0:1]
            hxy = values[1:2]
            hyy = values[2:3]
            state = []
            for c, start in enumerate((1.0, 0.0, 0.0, 1.0)):
                row = jnp.full((1, n), start, F32)
                if turn:
                    row = jnp.where(plane == 0, row, inbox_ref[pl.ds(4 * g + c, 1), pl.ds(at, n)])
                state.append(row)
            a11, a12, a21, a22 = state
            for c, value in enumerate(
                (
                    a11 - LENS_WEIGHT * (hxx * a11 + hxy * a21),
                    a12 - LENS_WEIGHT * (hxx * a12 + hxy * a22),
                    a21 - LENS_WEIGHT * (hxy * a11 + hyy * a21),
                    a22 - LENS_WEIGHT * (hxy * a12 + hyy * a22),
                )
            ):
                out_ref[pl.ds(4 * g + c, 1), pl.ds(at, n)] = value

        lookup(geo_ref, tab_ref, emit, tile_rows=tile_rows, turn=turn)

    @pl.when(jnp.logical_not(active))
    def _():
        out_ref[...] = jnp.zeros(out_ref.shape, F32)


def gather_kernel(*refs, planes, turns):
    *turn_refs, out_ref = refs
    plane = lax.axis_index("plane")
    group = turn_refs[0].shape[0] // 2
    groups = out_ref.shape[1] // group
    for p in range(planes):

        @pl.when(plane == p)
        def _():
            for j in range(groups):
                place = turn_refs[p + j]
                bend = turn_refs[turns + p + j]
                for i in range(group):
                    out_ref[0, j * group + i, 0:2, :] = place[2 * i : 2 * i + 2, :]
                    out_ref[0, j * group + i, 2:6, :] = bend[4 * i : 4 * i + 4, :]


def swapped(piece, e):
    tiles = lax.axis_size("tile")
    return lax.ppermute(piece, "tile", [(i, i ^ e) for i in range(tiles)])


def per_device(block_dest, particle_cell, particle_offset, particle_mass, ray_cell, ray_offset):
    tiles = lax.axis_size("tile")
    planes = lax.axis_size("plane")
    tile_rows = NG // tiles
    tile_now = lax.axis_index("tile")
    plane_now = lax.axis_index("plane")
    blocks = particle_cell.shape[1]
    block_len = particle_cell.shape[2]
    cap = 2 * blocks // tiles
    win = 3 * tile_rows

    outgoing = pl.pallas_call(
        route_kernel,
        out_shape=jax.ShapeDtypeStruct((tiles * 4 * cap, block_len), F32),
        in_specs=[hbm_spec()] * 4,
        out_specs=vmem_spec(),
        scratch_shapes=[
            pltpu.SMEM((blocks,), jnp.int32),
            VMEM(particle_cell.shape, jnp.int32),
            VMEM(particle_offset.shape, F32),
            VMEM(particle_mass.shape, F32),
            pltpu.SMEM((tiles,), jnp.int32),
            pltpu.SemaphoreType.DMA((4,)),
        ],
        compiler_params=params(58),
        name="route",
    )(block_dest.reshape(-1), particle_cell, particle_offset, particle_mass)
    incoming = lax.all_to_all(
        outgoing.reshape(tiles, 4 * cap, block_len), "tile", split_axis=0, concat_axis=0, tiled=True
    )

    v_hi, v_lo, u_hi, u_lo = pl.pallas_call(
        tables_kernel,
        out_shape=(
            jax.ShapeDtypeStruct((NP, NG), BF16),
            jax.ShapeDtypeStruct((NP, NG), BF16),
            jax.ShapeDtypeStruct((2 * win, NP), BF16),
            jax.ShapeDtypeStruct((2 * win, NP), BF16),
        ),
        in_specs=[],
        out_specs=(vmem_spec(),) * 4,
        compiler_params=params(12),
        name="tables",
    )()

    scaling = math.sqrt(tile_rows * NG / (BLOCKS_DEV * block_len))
    rows_acc = -(-(tile_rows + 1) // 16) * 16
    canvas_rows = tile_rows + 8
    canvas = pl.pallas_call(
        lambda a, b, c: deposit_kernel(a, b, c, scaling=scaling, tile_rows=tile_rows),
        out_shape=jax.ShapeDtypeStruct((canvas_rows, NG), F32),
        in_specs=[vmem_spec()],
        out_specs=vmem_spec(),
        scratch_shapes=[VMEM((4 * rows_acc, NG), F32)],
        compiler_params=params(12),
        name="deposit",
    )(incoming)

    near = [swapped(canvas, e) for e in range(2, tiles, 2)]
    v_hi, v_lo, u_hi, u_lo, *near = lax.optimization_barrier((v_hi, v_lo, u_hi, u_lo, *near))
    near = [canvas] + near
    canvases = [None] * tiles
    for d, piece in enumerate(near):
        canvases[2 * d] = piece
        canvases[2 * d + 1] = swapped(piece, 1)

    shape = jax.ShapeDtypeStruct
    part, tab_a, ba, window, corner = pl.pallas_call(
        lambda *refs: fields_kernel(refs[:tiles], *refs[tiles:], tile_rows=tile_rows),
        out_shape=(
            shape((2, tile_rows, NG), F32),
            shape((win // SUB, 2, SUB, 3 * NG), BF16),
            shape((2 * win, NP), F32),
            shape((win, NG), F32),
            shape((8, 128), F32),
        ),
        in_specs=[vmem_spec()] * (tiles + 4),
        out_specs=(vmem_spec(),) * 5,
        scratch_shapes=[
            VMEM((NG + 2 * tile_rows, NG), F32),
            VMEM((NG, NG), BF16),
            VMEM((NG, NG), BF16),
            VMEM((2 * win, NP), BF16),
            VMEM((2 * win, NP), BF16),
        ],
        compiler_params=params(24),
        name="fields",
    )(*canvases, v_hi, v_lo, u_hi, u_lo)
    lens, tab_h = pl.pallas_call(
        lambda *refs: second_kernel(*refs, tile_rows=tile_rows),
        out_shape=(
            shape((1, 5, tile_rows, NG), F32),
            shape((win // SUB, 3, SUB, 3 * NG), BF16),
        ),
        in_specs=[vmem_spec()] * 6,
        out_specs=(vmem_spec(),) * 2,
        scratch_shapes=[VMEM((3 * win, NP), BF16), VMEM((3 * win, NP), BF16)],
        compiler_params=params(16),
        name="second",
    )(ba, window, corner, part, v_hi, v_lo)

    batches = ray_cell.shape[0]
    rays = ray_cell.shape[1]
    groups_b = batches // GROUP
    ring = [(i, (i + 1) % planes) for i in range(planes)]
    turns = groups_b + planes - 1
    positions = []
    bends = []
    inbox = ()
    inbox_a = ()
    for turn in range(turns):
        place, geo = pl.pallas_call(
            lambda *refs, turn=turn: move_kernel(*refs, tile_rows=tile_rows, turn=turn),
            out_shape=(shape((2 * GROUP, rays), F32), shape((4 * GROUP, rays), F32)),
            in_specs=[vmem_spec()] * (len(inbox) + 3),
            out_specs=(vmem_spec(),) * 2,
            compiler_params=params(16),
            name=f"move{turn}",
        )(*inbox, ray_cell, ray_offset, tab_a)
        if turn < turns - 1:
            inbox = (lax.ppermute(place, "plane", ring),)
        bend = pl.pallas_call(
            lambda *refs, turn=turn: bend_kernel(
                *refs, groups=groups_b, tile_rows=tile_rows, turn=turn
            ),
            out_shape=shape((4 * GROUP, rays), F32),
            in_specs=[vmem_spec()] * (len(inbox_a) + 2),
            out_specs=vmem_spec(),
            compiler_params=params(16),
            name=f"bend{turn}",
        )(geo, tab_h, *inbox_a)
        if turn < turns - 1:
            placed, tied = lax.optimization_barrier((inbox[0], bend))
            inbox = (placed,)
            inbox_a = (lax.ppermute(tied, "plane", ring),)
        positions.append(place)
        bends.append(bend)
    ray_maps = pl.pallas_call(
        lambda *refs: gather_kernel(*refs, planes=planes, turns=turns),
        out_shape=shape((1, batches, 6, rays), F32),
        in_specs=[vmem_spec()] * (2 * turns),
        out_specs=vmem_spec(),
        compiler_params=params(8),
        name="gather",
    )(*positions, *bends)
    return (lens, ray_maps)


def solution(mesh):
    return jax.shard_map(
        per_device,
        mesh=mesh,
        in_specs=(
            P("plane", "tile", None),
            P("plane", "tile", None),
            P("plane", None, "tile", None),
            P("plane", "tile", None),
            P(None, "tile"),
            P(None, None, "tile"),
        ),
        out_specs=(P("plane", None, "tile", None), P("plane", None, None, "tile")),
        check_vma=False,
    )
```

```python
import math

import jax
import jax.numpy as jnp
from jax import lax
from jax.experimental import pallas as pl
from jax.experimental.pallas import tpu as pltpu
from jax.sharding import PartitionSpec as P

NG = 512
NP = 2 * NG
HALF = NP // 2
BLOCKS_DEV = 64

LENS_WEIGHT = 0.15
SCREEN_SCALE = 0.5
MU2 = (SCREEN_SCALE * 2.0 * math.pi / NP) ** 2
WAVE = 2.0 * math.pi / NP
F32 = jnp.float32
BF16 = jnp.bfloat16
VMEM = pltpu.VMEM
RAY_CHUNK = 1024
GROUP = 2
SUB = 16
TIERS = (5, 6)
STEP = 4


def vmem_spec():
    return pl.BlockSpec(memory_space=pltpu.VMEM)


def hbm_spec():
    return pl.BlockSpec(memory_space=pltpu.HBM)


def params(mib):
    return pltpu.CompilerParams(vmem_limit_bytes=mib * 1024 * 1024)


def smem_spec():
    return pl.BlockSpec(memory_space=pltpu.SMEM)


def split(x):
    hi = x.astype(BF16)
    return hi, (x - hi.astype(F32)).astype(BF16)


def dot_nt(a, b):
    return lax.dot_general(a, b, (((1,), (1,)), ((), ())), preferred_element_type=F32)


def dot_nn(a, b):
    return lax.dot_general(a, b, (((1,), (0,)), ((), ())), preferred_element_type=F32)


def route_kernel(dest_hbm, cell_hbm, offset_hbm, mass_hbm, out_ref, dest_ref, cell_ref, offset_ref, mass_ref, count_ref, sems):
    copies = [
        pltpu.make_async_copy(src, dst, sems.at[i])
        for i, (src, dst) in enumerate(
            (
                (dest_hbm, dest_ref),
                (cell_hbm, cell_ref),
                (offset_hbm, offset_ref),
                (mass_hbm, mass_ref),
            )
        )
    ]
    for copy in copies:
        copy.start()
    tiles = count_ref.shape[0]
    blocks = cell_ref.shape[1]
    cap = out_ref.shape[0] // (4 * tiles)
    out_ref[...] = jnp.zeros(out_ref.shape, F32)
    for t in range(tiles):
        count_ref[t] = 0
    for copy in copies:
        copy.wait()

    def place(i, carry):
        dest = dest_ref[i]
        rank = count_ref[dest]
        count_ref[dest] = rank + 1
        row = dest * (4 * cap) + rank
        out_ref[pl.ds(row, 1), :] = cell_ref[0, pl.ds(i, 1), :].astype(F32)
        out_ref[pl.ds(row + cap, 1), :] = offset_ref[0, 0, pl.ds(i, 1), :]
        out_ref[pl.ds(row + 2 * cap, 1), :] = offset_ref[0, 1, pl.ds(i, 1), :]
        out_ref[pl.ds(row + 3 * cap, 1), :] = mass_ref[0, pl.ds(i, 1), :]
        return carry

    lax.fori_loop(0, blocks, place, 0)


def deposit_kernel(in_ref, out_ref, acc_ref, *, scaling, tile_rows):
    tiles = in_ref.shape[0]
    cap = in_ref.shape[1] // 4
    lanes = in_ref.shape[2]
    group = min(8, cap)
    rows = -(-(tile_rows + 1) // 16) * 16
    acc_ref[...] = jnp.zeros(acc_ref.shape, F32)
    row_iota = lax.broadcasted_iota(jnp.int32, (rows, lanes), 0).astype(F32).astype(BF16)
    col_iota = (lax.broadcasted_iota(jnp.int32, (NG, lanes), 0) - NG // 2).astype(F32).astype(BF16)
    zero = jnp.zeros((), BF16)
    one = jnp.ones((), BF16)

    def step(src, start):
        pieces_r = []
        pieces_c = []
        for j in range(start, start + group):
            cell = in_ref[src, pl.ds(j, 1), :].astype(jnp.int32)
            frac_r = in_ref[src, pl.ds(cap + j, 1), :]
            frac_c = in_ref[src, pl.ds(2 * cap + j, 1), :]
            mass = in_ref[src, pl.ds(3 * cap + j, 1), :]
            row_id = (cell // NG).astype(F32)
            col_id = (cell % NG - NG // 2).astype(F32).astype(BF16)
            first = row_iota == row_id.astype(BF16)
            second = row_iota == (row_id + 1.0).astype(BF16)
            upper = mass * (1.0 - frac_r)
            lower = mass * frac_r
            rows_now = []
            for side in (1.0 - frac_c, frac_c):
                a_hi, a_lo = split(upper * side)
                b_hi, b_lo = split(lower * side)
                rows_now.append(jnp.where(first, a_hi, jnp.where(second, b_hi, zero)))
                rows_now.append(jnp.where(first, a_lo, jnp.where(second, b_lo, zero)))
            pieces_r.append(jnp.concatenate(rows_now, axis=0))
            pieces_c.append(jnp.where(col_iota == col_id, one, zero))
        acc_ref[...] += dot_nt(jnp.concatenate(pieces_r, axis=1), jnp.concatenate(pieces_c, axis=1))

    def per_source(src, carry):
        step(src, 0)
        for start in range(group, cap, group):
            block = in_ref[src, pl.ds(3 * cap + start, group), :]

            @pl.when(jnp.max(jnp.abs(block)) > 0.0)
            def _():
                step(src, start)

        return carry

    lax.fori_loop(0, tiles, per_source, 0)
    near = acc_ref[0:rows, :] + acc_ref[rows : 2 * rows, :]
    far = acc_ref[2 * rows : 3 * rows, :] + acc_ref[3 * rows : 4 * rows, :]
    lane = lax.broadcasted_iota(jnp.int32, (rows, NG), 1)
    total = (near + jnp.where(lane == 0, 0.0, pltpu.roll(far, 1, 1))) * scaling
    out_ref[...] = total[0 : out_ref.shape[0], :]


def unit_circle(left, right):
    turn = (left * right % NP).astype(F32) * WAVE
    return jnp.cos(turn), jnp.sin(turn)


def tables_kernel(v_hi_ref, v_lo_ref, u_hi_ref, u_lo_ref):
    lanes = 128
    fine = 32
    shape = (HALF // fine, lanes)
    coarse_c, coarse_s = unit_circle(
        fine * lax.broadcasted_iota(jnp.int32, shape, 0), lax.broadcasted_iota(jnp.int32, shape, 1)
    )
    shape = (fine, lanes)
    fine_c, fine_s = unit_circle(
        lax.broadcasted_iota(jnp.int32, shape, 0), lax.broadcasted_iota(jnp.int32, shape, 1)
    )
    parity = (1 - 2 * (lax.broadcasted_iota(jnp.int32, shape, 1) % 2)).astype(F32)
    first = lax.broadcasted_iota(jnp.int32, shape, 0) == 0
    for a in range(HALF // fine):
        ca = coarse_c[a : a + 1, :]
        sa = coarse_s[a : a + 1, :]
        base_cos = fine_c * ca - fine_s * sa
        base_sin = fine_s * ca + fine_c * sa
        k_index = a * fine + lax.broadcasted_iota(jnp.int32, shape, 0)
        for j in range(NG // lanes):
            q_cos, q_sin = 1.0, 0.0
            if j:
                step = NP // math.gcd(NP, lanes * j)
                turn = (k_index * (lanes * j)) % NP
                q_cos = jnp.ones(shape, F32)
                q_sin = jnp.zeros(shape, F32)
                for q in range(1, step):
                    angle = 2.0 * math.pi * q / step
                    hit = turn == q * (NP // step)
                    q_cos = jnp.where(hit, math.cos(angle), q_cos)
                    q_sin = jnp.where(hit, math.sin(angle), q_sin)
            cos_now = base_cos * q_cos - base_sin * q_sin
            sin_now = base_sin * q_cos + base_cos * q_sin
            if a == 0:
                sin_now = jnp.where(first, parity, sin_now)
            for at, value in ((0, cos_now), (HALF, sin_now)):
                hi, lo = split(value)
                v_hi_ref[at + a * fine : at + (a + 1) * fine, j * lanes : (j + 1) * lanes] = hi
                v_lo_ref[at + a * fine : at + (a + 1) * fine, j * lanes : (j + 1) * lanes] = lo
    win = u_hi_ref.shape[0] // 2
    fine = 16
    shape = (fine, HALF)
    fine_c, fine_s = unit_circle(
        lax.broadcasted_iota(jnp.int32, shape, 0), lax.broadcasted_iota(jnp.int32, shape, 1)
    )
    lane = lax.broadcasted_iota(jnp.int32, shape, 1)
    wave = lane.astype(F32) * WAVE
    parity = (1 - 2 * (lax.broadcasted_iota(jnp.int32, shape, 0) % 2)).astype(F32)
    for a in range(win // fine):
        ca, sa = unit_circle(jnp.full((1, HALF), a * fine, jnp.int32), lane[0:1])
        w_cos = fine_c * ca - fine_s * sa
        w_sin = fine_s * ca + fine_c * sa
        for rows, cols, value in (
            (0, 0, w_cos),
            (0, HALF, jnp.where(lane == 0, parity, w_sin)),
            (win, 0, -wave * w_sin),
            (win, HALF, wave * w_cos),
        ):
            hi, lo = split(value)
            u_hi_ref[rows + a * fine : rows + (a + 1) * fine, cols : cols + HALF] = hi
            u_lo_ref[rows + a * fine : rows + (a + 1) * fine, cols : cols + HALF] = lo


def fields_kernel(
    canvas_refs,
    v_hi_ref,
    v_lo_ref,
    u_hi_ref,
    u_lo_ref,
    lens_ref,
    tab_ref,
    ba_ref,
    window_ref,
    corner_ref,
    dens_ref,
    dens_hi_ref,
    dens_lo_ref,
    l_hi_ref,
    l_lo_ref,
    *,
    tile_rows,
):
    tile = lax.axis_index("tile")
    tiles = len(canvas_refs)
    win = 3 * tile_rows
    pad = tile_rows
    zeros = jnp.zeros((pad, NG), F32)
    dens_ref[0:pad, :] = zeros
    dens_ref[pad + NG : pad + NG + pad, :] = zeros
    for e, src in enumerate(canvas_refs):
        row = pl.multiple_of(pad + jnp.bitwise_xor(tile, e) * tile_rows, 8)
        dens_ref[pl.ds(row, tile_rows), :] = src[0:tile_rows, :]
    for e, src in enumerate(canvas_refs):
        below = jnp.bitwise_xor(tile, e) + 1
        row = pl.multiple_of(pad + below * tile_rows, 8)
        dens_ref[pl.ds(row, 8), :] += jnp.where(below < tiles, src[tile_rows : tile_rows + 8, :], 0.0)
    d_hi, d_lo = split(dens_ref[pad : pad + NG, :])
    dens_hi_ref[...] = d_hi
    dens_lo_ref[...] = d_lo

    half_lane = lax.broadcasted_iota(jnp.int32, (1, HALF), 1).astype(F32) * WAVE
    origin = (tile - 1) * tile_rows + NP
    turn = (lax.broadcasted_iota(jnp.int32, (1, HALF), 1) * origin % NP).astype(F32) * WAVE
    turn_cos = jnp.cos(turn)
    turn_sin = jnp.sin(turn)
    lane = lax.broadcasted_iota(jnp.int32, (1, NP), 1)
    k_slot = jnp.where(lane < HALF, lane, jnp.where(lane == HALF, HALF, lane - HALF))
    kx = k_slot.astype(F32) * WAVE
    kx2 = kx * kx
    edge_k = (lane == 0) | (lane == HALF)
    weight_k = jnp.where(edge_k, 1.0, 2.0)
    block = 1024

    def channel_block(i, corner):
        at = pl.multiple_of(i * block, block)
        v_hi = v_hi_ref[pl.ds(at, block), :]
        v_lo = v_lo_ref[pl.ds(at, block), :]
        dh = dens_hi_ref[...]
        first = dot_nt(v_hi, dh) + dot_nt(v_lo, dh) + dot_nt(v_hi, dens_lo_ref[...])
        f_hi, f_lo = split(first)
        spec = (
            dot_nt(f_hi, v_hi_ref[...]) + dot_nt(f_lo, v_hi_ref[...]) + dot_nt(f_hi, v_lo_ref[...])
        )
        chan = at + lax.broadcasted_iota(jnp.int32, (block, 1), 0)
        l_slot = jnp.where(chan < HALF, chan, jnp.where(chan == HALF, HALF, chan - HALF))
        ky = l_slot.astype(F32) * WAVE
        weight_l = jnp.where((chan == 0) | (chan == HALF), 1.0, 2.0)
        scale = (weight_l * (-2.0 / (NP * NP))) * weight_k
        pot = spec * (scale / (kx2 + ky * ky + MU2))
        corner = jnp.where(i == HALF // block, pot[HALF % block : HALF % block + 1, HALF : HALF + 1], corner)
        pot_c = pot[:, 0:HALF]
        pot_s = pot[:, HALF:NP]
        turned = jnp.concatenate(
            [pot_c * turn_cos + pot_s * turn_sin, pot_s * turn_cos - pot_c * turn_sin], axis=1
        )
        p_hi, p_lo = split(turned)
        uh = u_hi_ref[...]
        ba_ref[:, pl.ds(at, block)] = (
            dot_nt(uh, p_hi) + dot_nt(u_lo_ref[...], p_hi) + dot_nt(uh, p_lo)
        )
        return corner

    corner = lax.fori_loop(0, NP // block, channel_block, jnp.zeros((1, 1), F32))

    row_at = lax.broadcasted_iota(jnp.int32, (win, 1), 0)
    grid_row = (tile - 1) * tile_rows + row_at
    inside = ((grid_row >= 0) & (grid_row < NG)).astype(F32)
    b_all = ba_ref[0:win, :] * inside
    a_all = ba_ref[win : 2 * win, :] * inside
    ba_ref[0:win, :] = b_all
    ba_ref[win : 2 * win, :] = a_all
    window_ref[...] = dens_ref[pl.ds(pl.multiple_of(tile * tile_rows, 8), win), :]
    corner_ref[...] = jnp.broadcast_to(corner * (-math.pi * math.pi), corner_ref.shape)
    slope = jnp.concatenate([half_lane * b_all[:, HALF:NP], -half_lane * b_all[:, 0:HALF]], axis=1)
    for f, value in enumerate((a_all, slope)):
        hi, lo = split(value)
        l_hi_ref[f * win : (f + 1) * win, :] = hi
        l_lo_ref[f * win : (f + 1) * win, :] = lo
    finish(2, l_hi_ref, l_lo_ref, v_hi_ref, v_lo_ref, None, lens_ref, tab_ref, tile_rows)


def finish(count, l_hi_ref, l_lo_ref, v_hi_ref, v_lo_ref, extra_ref, lens_ref, tab_ref, tile_rows):
    win = 3 * tile_rows
    shape = (win // SUB, SUB, NG)
    vh = v_hi_ref[...]
    out = dot_nn(l_hi_ref[...], vh) + dot_nn(l_lo_ref[...], vh) + dot_nn(l_hi_ref[...], v_lo_ref[...])
    at = lens_ref.shape[-3] - count
    for f in range(count):
        value = out[f * win : (f + 1) * win, :]
        if f == 0 and extra_ref is not None:
            value = value + 2.0 * extra_ref[...]
        lens_ref[..., at + f, :, :] = value[tile_rows : 2 * tile_rows, :].reshape(
            (1,) * (len(lens_ref.shape) - 3) + (tile_rows, NG)
        )
        hi, lo = split(value)
        tab_ref[:, f, :, 0:NG] = hi.reshape(shape)
        tab_ref[:, f, :, NG : 2 * NG] = lo.reshape(shape)
        tab_ref[:, f, :, 2 * NG : 3 * NG] = hi.reshape(shape)


def second_kernel(
    ba_ref,
    window_ref,
    corner_ref,
    part_ref,
    v_hi_ref,
    v_lo_ref,
    lens_ref,
    tab_ref,
    l_hi_ref,
    l_lo_ref,
    *,
    tile_rows,
):
    tile = lax.axis_index("tile")
    win = 3 * tile_rows
    lens_ref[0, 0:2] = part_ref[...]
    row_at = lax.broadcasted_iota(jnp.int32, (win, 1), 0)
    grid_row = (tile - 1) * tile_rows + row_at
    inside = ((grid_row >= 0) & (grid_row < NG)).astype(F32)
    corner_col = inside * (1 - 2 * (row_at % 2)).astype(F32) * corner_ref[0:1, 0:1]
    lane = lax.broadcasted_iota(jnp.int32, (1, NP), 1)
    slot = jnp.where(lane < HALF, lane, jnp.where(lane == HALF, HALF, lane - HALF))
    ky2 = (slot.astype(F32) * WAVE) * (slot.astype(F32) * WAVE)
    lane_half = lax.broadcasted_iota(jnp.int32, (1, HALF), 1)
    half_lane = lane_half.astype(F32) * WAVE
    b_all = ba_ref[0:win, :]
    a_cos = ba_ref[win : 2 * win, 0:HALF]
    a_sin = ba_ref[win : 2 * win, HALF:NP]
    mixed = jnp.concatenate(
        [half_lane * a_sin, jnp.where(lane_half == 0, corner_col, -half_lane * a_cos)], axis=1
    )
    for f, value in enumerate(((MU2 + ky2) * b_all, mixed, -ky2 * b_all)):
        hi, lo = split(value)
        l_hi_ref[f * win : (f + 1) * win, :] = hi
        l_lo_ref[f * win : (f + 1) * win, :] = lo
    finish(3, l_hi_ref, l_lo_ref, v_hi_ref, v_lo_ref, window_ref, lens_ref, tab_ref, tile_rows)


def lookup(geo_ref, tab_ref, emit, *, tile_rows, turn):
    chunks, fields, _, _ = tab_ref.shape
    group = geo_ref.shape[0] // 4
    rays = geo_ref.shape[1]
    n = min(RAY_CHUNK, rays)
    per = rays // n
    zero = jnp.zeros((), BF16)
    win = chunks * SUB
    least = float(win)
    most = 0.0
    for g in range(group):
        row_id = geo_ref[4 * g : 4 * g + 1, :]
        least = jnp.minimum(least, jnp.min(row_id))
        most = jnp.maximum(most, jnp.max(row_id))
    low = jnp.clip(least.astype(jnp.int32), 0, win - 1) // SUB
    high = jnp.clip(most.astype(jnp.int32) + 1, 0, win - 1) // SUB
    needed = high - low + 1
    tiers = sorted({min(t, chunks) for t in TIERS})

    def with_tier(tier, passes):
        col_iota = (lax.broadcasted_iota(jnp.int32, (NG, n), 0) - NG // 2).astype(F32).astype(BF16)
        row_iota = lax.broadcasted_iota(jnp.int32, (tier * SUB, n), 0).astype(F32)

        def chunk(i, carry):
            g = i // per
            at = pl.multiple_of((i % per) * n, n)
            row_id = geo_ref[pl.ds(4 * g, 1), pl.ds(at, n)]
            frac_row = geo_ref[pl.ds(4 * g + 1, 1), pl.ds(at, n)]
            col_floor = geo_ref[pl.ds(4 * g + 2, 1), pl.ds(at, n)]
            frac_col = geo_ref[pl.ds(4 * g + 3, 1), pl.ds(at, n)]
            far = 4.0 * NG
            c0 = jnp.where((col_floor >= 0.0) & (col_floor < NG), col_floor - NG // 2, far)
            c1 = jnp.where(
                (col_floor >= -1.0) & (col_floor < NG - 1.0), col_floor + (1.0 - NG // 2), far
            )
            here = col_iota == c0.astype(BF16)
            there = col_iota == c1.astype(BF16)
            g0_hi, g0_lo = split(1.0 - frac_col)
            g1_hi, g1_lo = split(frac_col)
            w_hi = jnp.where(here, g0_hi, jnp.where(there, g1_hi, zero))
            w_lo = jnp.where(here, g0_lo, jnp.where(there, g1_lo, zero))
            w = jnp.concatenate([w_hi, w_hi, w_lo], axis=0)

            def rows_from(start, floor):
                here_row = row_id - (start * SUB).astype(F32)
                row_w = jnp.where(row_iota == here_row, 1.0 - frac_row, 0.0) + jnp.where(
                    row_iota == here_row + 1.0, frac_row, 0.0
                )
                if floor is not None:
                    row_w = jnp.where(row_iota >= floor, row_w, 0.0)
                table = tab_ref[pl.ds(start, tier)].reshape(tier * fields * SUB, 3 * NG)
                along = dot_nn(table, w).reshape(tier, fields, SUB, n)
                values = jnp.sum(along * row_w.reshape(tier, 1, SUB, n), axis=0)
                return jnp.sum(values, axis=1)

            if passes is None:
                values = rows_from(jnp.minimum(low, chunks - tier), None)
            else:

                def one_pass(q, total):
                    begin = low + q * tier
                    start = jnp.minimum(begin, chunks - tier)
                    return total + rows_from(start, ((begin - start) * SUB).astype(F32))

                values = lax.fori_loop(0, passes, one_pass, jnp.zeros((fields, n), F32))
            emit(g, at, n, values)
            return carry

        lax.fori_loop(0, group * per, chunk, 0)

    still = (2 * tile_rows + 1) // SUB - tile_rows // SUB + 1
    if turn == 0:
        with_tier(still, None)
        return
    if turn > 1:
        tiers = [t for t in tiers if t > still] or tiers[-1:]
    floor = 0
    for tier in tiers:
        pl.when((needed > floor) & (needed <= tier))(lambda tier=tier: with_tier(tier, None))
        floor = tier
    if floor < chunks:
        pl.when(needed > floor)(lambda: with_tier(STEP, (needed + STEP - 1) // STEP))


def move_kernel(*refs, tile_rows, turn):
    if turn:
        inbox_ref, cell_ref, offset_ref, tab_ref, out_ref, geo_ref = refs
    else:
        cell_ref, offset_ref, tab_ref, out_ref, geo_ref = refs
    tile = lax.axis_index("tile")
    plane = lax.axis_index("plane")
    group = geo_ref.shape[0] // 4
    groups = cell_ref.shape[0] // group
    which = turn - plane
    active = (which >= 0) & (which < groups)
    span = float(tile_rows - 1)

    def came(g, axis, at, n):
        if not turn:
            return jnp.zeros((1, n), F32)
        return jnp.where(plane == 0, 0.0, inbox_ref[pl.ds(2 * g + axis, 1), pl.ds(at, n)])

    @pl.when(active)
    def _():
        rays = out_ref.shape[1]
        for g in range(group):
            batch = which * group + g
            cell = cell_ref[pl.ds(batch, 1), :]
            base_row = (tile * tile_rows + cell // NG).astype(F32) + offset_ref[0, pl.ds(batch, 1), :]
            base_col = (cell % NG).astype(F32) + offset_ref[1, pl.ds(batch, 1), :]
            row_pos = base_row + span * jnp.tanh(came(g, 0, 0, rays) / span)
            col_pos = base_col + span * jnp.tanh(came(g, 1, 0, rays) / span)
            row_floor = jnp.floor(row_pos)
            col_floor = jnp.floor(col_pos)
            geo_ref[4 * g : 4 * g + 1, :] = row_floor - ((tile - 1) * tile_rows).astype(F32)
            geo_ref[4 * g + 1 : 4 * g + 2, :] = row_pos - row_floor
            geo_ref[4 * g + 2 : 4 * g + 3, :] = col_floor
            geo_ref[4 * g + 3 : 4 * g + 4, :] = col_pos - col_floor

        def emit(g, at, n, values):
            for axis in (0, 1):
                out_ref[pl.ds(2 * g + axis, 1), pl.ds(at, n)] = (
                    came(g, axis, at, n) - LENS_WEIGHT * values[axis : axis + 1]
                )

        lookup(geo_ref, tab_ref, emit, tile_rows=tile_rows, turn=turn)

    @pl.when(jnp.logical_not(active))
    def _():
        out_ref[...] = jnp.zeros(out_ref.shape, F32)
        geo_ref[...] = jnp.zeros(geo_ref.shape, F32)


def bend_kernel(*refs, groups, tile_rows, turn):
    if turn:
        geo_ref, tab_ref, inbox_ref, out_ref = refs
    else:
        geo_ref, tab_ref, out_ref = refs
    plane = lax.axis_index("plane")
    which = turn - plane
    active = (which >= 0) & (which < groups)

    @pl.when(active)
    def _():
        def emit(g, at, n, values):
            hxx = values[0:1]
            hxy = values[1:2]
            hyy = values[2:3]
            state = []
            for c, start in enumerate((1.0, 0.0, 0.0, 1.0)):
                row = jnp.full((1, n), start, F32)
                if turn:
                    row = jnp.where(plane == 0, row, inbox_ref[pl.ds(4 * g + c, 1), pl.ds(at, n)])
                state.append(row)
            a11, a12, a21, a22 = state
            for c, value in enumerate(
                (
                    a11 - LENS_WEIGHT * (hxx * a11 + hxy * a21),
                    a12 - LENS_WEIGHT * (hxx * a12 + hxy * a22),
                    a21 - LENS_WEIGHT * (hxy * a11 + hyy * a21),
                    a22 - LENS_WEIGHT * (hxy * a12 + hyy * a22),
                )
            ):
                out_ref[pl.ds(4 * g + c, 1), pl.ds(at, n)] = value

        lookup(geo_ref, tab_ref, emit, tile_rows=tile_rows, turn=turn)

    @pl.when(jnp.logical_not(active))
    def _():
        out_ref[...] = jnp.zeros(out_ref.shape, F32)


def gather_kernel(*refs, planes, turns):
    *turn_refs, out_ref = refs
    plane = lax.axis_index("plane")
    group = turn_refs[0].shape[0] // 2
    groups = out_ref.shape[1] // group
    for p in range(planes):

        @pl.when(plane == p)
        def _():
            for j in range(groups):
                place = turn_refs[p + j]
                bend = turn_refs[turns + p + j]
                for i in range(group):
                    out_ref[0, j * group + i, 0:2, :] = place[2 * i : 2 * i + 2, :]
                    out_ref[0, j * group + i, 2:6, :] = bend[4 * i : 4 * i + 4, :]


def swapped(piece, e):
    tiles = lax.axis_size("tile")
    return lax.ppermute(piece, "tile", [(i, i ^ e) for i in range(tiles)])


def per_device(block_dest, particle_cell, particle_offset, particle_mass, ray_cell, ray_offset):
    tiles = lax.axis_size("tile")
    planes = lax.axis_size("plane")
    tile_rows = NG // tiles
    tile_now = lax.axis_index("tile")
    plane_now = lax.axis_index("plane")
    blocks = particle_cell.shape[1]
    block_len = particle_cell.shape[2]
    cap = 2 * blocks // tiles
    win = 3 * tile_rows

    outgoing = pl.pallas_call(
        route_kernel,
        out_shape=jax.ShapeDtypeStruct((tiles * 4 * cap, block_len), F32),
        in_specs=[hbm_spec()] * 4,
        out_specs=vmem_spec(),
        scratch_shapes=[
            pltpu.SMEM((blocks,), jnp.int32),
            VMEM(particle_cell.shape, jnp.int32),
            VMEM(particle_offset.shape, F32),
            VMEM(particle_mass.shape, F32),
            pltpu.SMEM((tiles,), jnp.int32),
            pltpu.SemaphoreType.DMA((4,)),
        ],
        compiler_params=params(58),
        name="route",
    )(block_dest.reshape(-1), particle_cell, particle_offset, particle_mass)
    incoming = lax.all_to_all(
        outgoing.reshape(tiles, 4 * cap, block_len), "tile", split_axis=0, concat_axis=0, tiled=True
    )

    v_hi, v_lo, u_hi, u_lo = pl.pallas_call(
        tables_kernel,
        out_shape=(
            jax.ShapeDtypeStruct((NP, NG), BF16),
            jax.ShapeDtypeStruct((NP, NG), BF16),
            jax.ShapeDtypeStruct((2 * win, NP), BF16),
            jax.ShapeDtypeStruct((2 * win, NP), BF16),
        ),
        in_specs=[],
        out_specs=(vmem_spec(),) * 4,
        compiler_params=params(12),
        name="tables",
    )()

    scaling = math.sqrt(tile_rows * NG / (BLOCKS_DEV * block_len))
    rows_acc = -(-(tile_rows + 1) // 16) * 16
    canvas_rows = tile_rows + 8
    canvas = pl.pallas_call(
        lambda a, b, c: deposit_kernel(a, b, c, scaling=scaling, tile_rows=tile_rows),
        out_shape=jax.ShapeDtypeStruct((canvas_rows, NG), F32),
        in_specs=[vmem_spec()],
        out_specs=vmem_spec(),
        scratch_shapes=[VMEM((4 * rows_acc, NG), F32)],
        compiler_params=params(12),
        name="deposit",
    )(incoming)

    near = [swapped(canvas, e) for e in range(2, tiles, 2)]
    v_hi, v_lo, u_hi, u_lo, *near = lax.optimization_barrier((v_hi, v_lo, u_hi, u_lo, *near))
    near = [canvas] + near
    canvases = [None] * tiles
    for d, piece in enumerate(near):
        canvases[2 * d] = piece
        canvases[2 * d + 1] = swapped(piece, 1)

    shape = jax.ShapeDtypeStruct
    part, tab_a, ba, window, corner = pl.pallas_call(
        lambda *refs: fields_kernel(refs[:tiles], *refs[tiles:], tile_rows=tile_rows),
        out_shape=(
            shape((2, tile_rows, NG), F32),
            shape((win // SUB, 2, SUB, 3 * NG), BF16),
            shape((2 * win, NP), F32),
            shape((win, NG), F32),
            shape((8, 128), F32),
        ),
        in_specs=[vmem_spec()] * (tiles + 4),
        out_specs=(vmem_spec(),) * 5,
        scratch_shapes=[
            VMEM((NG + 2 * tile_rows, NG), F32),
            VMEM((NG, NG), BF16),
            VMEM((NG, NG), BF16),
            VMEM((2 * win, NP), BF16),
            VMEM((2 * win, NP), BF16),
        ],
        compiler_params=params(36),
        name="fields",
    )(*canvases, v_hi, v_lo, u_hi, u_lo)
    lens, tab_h = pl.pallas_call(
        lambda *refs: second_kernel(*refs, tile_rows=tile_rows),
        out_shape=(
            shape((1, 5, tile_rows, NG), F32),
            shape((win // SUB, 3, SUB, 3 * NG), BF16),
        ),
        in_specs=[vmem_spec()] * 6,
        out_specs=(vmem_spec(),) * 2,
        scratch_shapes=[VMEM((3 * win, NP), BF16), VMEM((3 * win, NP), BF16)],
        compiler_params=params(16),
        name="second",
    )(ba, window, corner, part, v_hi, v_lo)

    batches = ray_cell.shape[0]
    rays = ray_cell.shape[1]
    groups_b = batches // GROUP
    ring = [(i, (i + 1) % planes) for i in range(planes)]
    turns = groups_b + planes - 1
    positions = []
    bends = []
    inbox = ()
    inbox_a = ()
    for turn in range(turns):
        place, geo = pl.pallas_call(
            lambda *refs, turn=turn: move_kernel(*refs, tile_rows=tile_rows, turn=turn),
            out_shape=(shape((2 * GROUP, rays), F32), shape((4 * GROUP, rays), F32)),
            in_specs=[vmem_spec()] * (len(inbox) + 3),
            out_specs=(vmem_spec(),) * 2,
            compiler_params=params(16),
            name=f"move{turn}",
        )(*inbox, ray_cell, ray_offset, tab_a)
        if turn < turns - 1:
            inbox = (lax.ppermute(place, "plane", ring),)
        bend = pl.pallas_call(
            lambda *refs, turn=turn: bend_kernel(
                *refs, groups=groups_b, tile_rows=tile_rows, turn=turn
            ),
            out_shape=shape((4 * GROUP, rays), F32),
            in_specs=[vmem_spec()] * (len(inbox_a) + 2),
            out_specs=vmem_spec(),
            compiler_params=params(16),
            name=f"bend{turn}",
        )(geo, tab_h, *inbox_a)
        if turn < turns - 1:
            placed, tied = lax.optimization_barrier((inbox[0], bend))
            inbox = (placed,)
            inbox_a = (lax.ppermute(tied, "plane", ring),)
        positions.append(place)
        bends.append(bend)
    ray_maps = pl.pallas_call(
        lambda *refs: gather_kernel(*refs, planes=planes, turns=turns),
        out_shape=shape((1, batches, 6, rays), F32),
        in_specs=[vmem_spec()] * (2 * turns),
        out_specs=vmem_spec(),
        compiler_params=params(8),
        name="gather",
    )(*positions, *bends)
    return (lens, ray_maps)


def solution(mesh):
    return jax.shard_map(
        per_device,
        mesh=mesh,
        in_specs=(
            P("plane", "tile", None),
            P("plane", "tile", None),
            P("plane", None, "tile", None),
            P("plane", "tile", None),
            P(None, "tile"),
            P(None, None, "tile"),
        ),
        out_specs=(P("plane", None, "tile", None), P("plane", None, None, "tile")),
        check_vma=False,
    )
```
